32 devices in a mesh: dp: 4 (over x, core), tp: 8 (over z, y).
Axes of the slice: x: 2, y: 2, z: 4, core: 2. Of those that a mesh axis runs over, the one named last changes fastest.
Arguments:
- layer_inputs: bfloat16 [2, 1536, 4608], P(None, 'dp'), may hold values from -120 to 120
- out_grad: bfloat16 [1536, 4608], P('dp'), may hold values from -6 to 6
- gain: float32 [2, 4608], replicated, may hold values from 0.5 to 1.5
- w_query: bfloat16 [2, 4608, 4096], P(None, None, 'tp'), may hold values from -0.09375 to 0.09375
- w_key: bfloat16 [2, 4608, 2048], P(None, None, 'tp'), may hold values from -0.09375 to 0.09375
- w_value: bfloat16 [2, 4608, 2048], P(None, None, 'tp'), may hold values from -0.09375 to 0.09375
- w_out: bfloat16 [2, 4096, 4608], P(None, 'tp'), may hold values from -0.09375 to 0.09375
- doc_lengths: int32 [4, 4], P('dp'), may hold values from 1 to 192, 384 in all within a row
- window_reach: int32 [2], replicated, may hold values from 48 to 384, as said below
Outputs:
- input_grad: bfloat16 [1536, 4608], P('dp')
- grad_w_query: float32 [2, 4608, 4096], P(None, 'dp', 'tp')
- grad_w_key: float32 [2, 4608, 2048], P(None, 'dp', 'tp')
- grad_w_value: float32 [2, 4608, 2048], P(None, 'dp', 'tp')
- grad_w_out: float32 [2, 4096, 4608], P(None, 'tp', 'dp')
- grad_gain: float32 [2, 4608], replicated
The draws below stay inside these ranges and needn't reach their ends.
Inputs may be any that keep to these rules, and one draw needn't show every extreme that they name: `doc_lengths`: the 4 lengths of a row fill its sequence's 384 positions in order; in every row the longest document has exactly 192 positions. `window_reach`: exactly one sublayer has reach 384 (it sees all earlier positions of its document); the other's reach is at most 192.
All inputs are finite; a program needn't handle non-finite values.
Results may differ from the reference program's by a relative error of at most 0.025.
Values may be sent and summed in bfloat16 or wider, within the bound.
No kernel may reach another device: no remote copies, remote signals or barrier semaphores. Data moves between devices by JAX's collectives and lax.ppermute only.
A program may use at most 192 MiB of HBM per device.

```python
import math
import jax
import jax.numpy as jnp
import numpy as np
from jax import lax

D = 4608
HEADS = 32
KV_HEADS = 16
HD = 128
SEQ_LEN = 384
LAYERS = 2
DOCS = 4
SEQUENCES = 4
TOKENS = 1536
N_DP = 4


def draw_layer_inputs(key, part):
    subkeys = jax.random.split(jax.random.fold_in(key, 11), 3)
    full_shape = (LAYERS, TOKENS, D)
    row_scale = jnp.exp(jax.random.uniform(subkeys[0], (LAYERS, TOKENS, 1), jnp.float32, 0.0, math.log(10.0)))
    col_scale = jnp.exp(jax.random.uniform(subkeys[1], (LAYERS, 1, D), jnp.float32, math.log(0.3), math.log(3.0)))
    entries = jnp.clip(jax.random.normal(subkeys[2], full_shape, jnp.float32), -4.0, 4.0)
    return (entries * row_scale * col_scale).astype(jnp.bfloat16)


def draw_window_reach(key, part):
    subkeys = jax.random.split(jax.random.fold_in(key, 23), 2)
    span = jax.random.randint(subkeys[0], (), SEQ_LEN // 8, SEQ_LEN // 2 + 1, jnp.int32)
    which = jax.random.randint(subkeys[1], (), 0, LAYERS, jnp.int32)
    layer_index = jnp.arange(LAYERS, dtype=jnp.int32)
    return jnp.where(layer_index == which, jnp.int32(SEQ_LEN), span).astype(jnp.int32)


def block_scale(stream_key, dims, pieces, smallest, top_value):
    def one(dim, blocks):
        steps = jax.random.uniform(jax.random.fold_in(jax.random.fold_in(stream_key, 6), dim), (blocks,), jnp.float32, smallest / len(pieces), top_value / len(pieces))
        return jnp.repeat(jnp.exp(steps), dims[dim] // blocks).reshape((-1,) + (1,) * (len(dims) - dim - 1))

    level = one(*pieces[0])
    for cut in pieces[1:]:
        level = level * one(*cut)
    return level


def profile(amount, total, bound, skew):
    portions = [(1 << 20) // math.isqrt(standing ** skew) + 1 for standing in range(2, amount + 1)]
    surplus, holding = total - bound - (amount - 1), [1] * (amount - 1)
    while surplus > 0:
        candidates = [i for i in range(amount - 1) if holding[i] < bound]
        pool, budget = sum([portions[i] for i in candidates]), surplus
        for i in candidates:
            more = min(bound - holding[i], max(1, budget * portions[i] // pool), surplus)
            holding[i] = holding[i] + more
            surplus = surplus - more
    return np.array([bound] + holding)


def ragged_sizes(stream_key, number_of, total, bound, lean):
    if number_of == 2:
        one = jax.random.randint(stream_key, (), max(1, total - bound), min(bound, total - 1) + 1)
        return jnp.stack([one, total - one])
    sizes = jnp.asarray(profile(number_of, total, bound, lean), jnp.int32)
    twos = (number_of - 1) // 2
    giver, sink = sizes[1:1 + 2 * twos:2], sizes[2:2 + 2 * twos:2]
    slack = jnp.minimum(giver - 1, bound - sink)
    moved = jax.random.randint(jax.random.fold_in(stream_key, 1), (twos,), 0, 1 << 20) % (slack + 1)
    sizes = sizes.at[1:1 + 2 * twos:2].set(giver - moved).at[2:2 + 2 * twos:2].set(sink + moved)
    return sizes[jax.random.permutation(jax.random.fold_in(stream_key, 2), number_of)]


def scatter_about(key, dims, scale, most, cuts=(), kind=jnp.bfloat16):
    values = scale * jax.random.normal(key, dims, jnp.float32)
    if cuts:
        values = values * block_scale(key, dims, cuts, -0.22, 0.18)
    return jnp.clip(values, -most, most).astype(kind)


def setup_inputs(seed: int = 0) -> dict:
    streams_of = jax.random.split(jax.random.key(seed), 10)
    layer_inputs = draw_layer_inputs(jax.random.fold_in(streams_of[9], 71), 0)
    out_grad = scatter_about(streams_of[1], (TOKENS, D), 1.0, 6.0, ((0, 4),))
    gain = jnp.clip(1.0 + 0.1 * jax.random.normal(streams_of[2], (LAYERS, D), jnp.float32), 0.5, 1.5)
    w_query = scatter_about(streams_of[3], (LAYERS, D, HEADS * HD), D ** -0.5, 0.09375, ((2, 8),))
    w_key = scatter_about(streams_of[4], (LAYERS, D, KV_HEADS * HD), D ** -0.5, 0.09375, ((2, 8),))
    w_value = scatter_about(streams_of[5], (LAYERS, D, KV_HEADS * HD), D ** -0.5, 0.09375, ((2, 8),))
    w_out = scatter_about(streams_of[6], (LAYERS, HEADS * HD, D), (HEADS * HD) ** -0.5, 0.09375, ((1, 8),))
    doc_lengths = jax.vmap(lambda own: ragged_sizes(own, DOCS, SEQ_LEN, SEQ_LEN // 2, 2))(jax.random.split(streams_of[7], SEQUENCES)).reshape((SEQUENCES, DOCS)).astype(jnp.int32)
    window_reach = draw_window_reach(jax.random.fold_in(streams_of[9], 71), 0)
    return {"layer_inputs": layer_inputs, "out_grad": out_grad, "gain": gain, "w_query": w_query, "w_key": w_key, "w_value": w_value, "w_out": w_out, "doc_lengths": doc_lengths, "window_reach": window_reach}


softcap = 50.0
epsilon = 1e-06

def rope_tables(length, head_width):
    half_width = head_width // 2
    frequencies = jnp.exp(-jnp.arange(half_width).astype(jnp.float32) * (2.0 * math.log(10000.0) / head_width))
    angles = jnp.arange(length).astype(jnp.float32)[:, None] * frequencies[None, :]
    return (jnp.cos(angles)[:, None, :], jnp.sin(angles)[:, None, :])

def rotate(values, cosine, sine_table):
    half_width = values.shape[-1] // 2
    first_half = values[..., :half_width]
    second_half = values[..., half_width:]
    return jnp.concatenate([first_half * cosine - second_half * sine_table, second_half * cosine + first_half * sine_table], axis=-1)

def unrotate(values, cosine, sine_table):
    half_width = values.shape[-1] // 2
    first_half = values[..., :half_width]
    second_half = values[..., half_width:]
    return jnp.concatenate([first_half * cosine + second_half * sine_table, second_half * cosine - first_half * sine_table], axis=-1)

def allowed_pairs(lengths_row, reach, length):
    doc_ends = jnp.cumsum(lengths_row.astype(jnp.int32))
    places = jnp.arange(length, dtype=jnp.int32)
    document = lax.optimization_barrier(jnp.sum((places[:, None] >= doc_ends[None, :]).astype(jnp.int32), axis=1))
    same_doc = document[:, None] == document[None, :]
    causal = places[None, :] <= places[:, None]
    in_window = places[:, None] - places[None, :] < reach.astype(jnp.int32)
    return same_doc & causal & in_window

def layer_backward(inputs, upstream, gain_row, query_weight, key_weight, value_weight, out_weight, lengths_row, reach):
    length = inputs.shape[0]
    cosine, sine_table = rope_tables(length, HD)
    score_scale = (D // HEADS) ** (-0.5)
    allowed = allowed_pairs(lengths_row, reach, length)
    matrix_rows = inputs.astype(jnp.float32)
    reciprocal = lax.rsqrt(lax.optimization_barrier(jnp.mean(matrix_rows * matrix_rows, axis=-1, keepdims=True)) + epsilon)
    unit_rows = matrix_rows * reciprocal
    normed = (unit_rows * gain_row).astype(jnp.bfloat16)
    queries = rotate(jnp.dot(normed, query_weight, preferred_element_type=jnp.float32).reshape(length, HEADS, HD), cosine, sine_table).astype(jnp.bfloat16)
    keys_rope = rotate(jnp.dot(normed, key_weight, preferred_element_type=jnp.float32).reshape(length, KV_HEADS, HD), cosine, sine_table).astype(jnp.bfloat16)
    values_cast = jnp.dot(normed, value_weight, preferred_element_type=jnp.float32).reshape(length, KV_HEADS, HD).astype(jnp.bfloat16)
    keys_shared = jnp.repeat(keys_rope, 2, axis=1).astype(jnp.float32)
    values_shared = jnp.repeat(values_cast, 2, axis=1).astype(jnp.float32)
    queries_float = queries.astype(jnp.float32)
    scores = jnp.einsum('thd,shd->hts', queries_float, keys_shared) * score_scale
    squashed = jnp.tanh(scores / softcap)
    raised = jnp.where(allowed[None], jnp.exp(softcap * squashed), 0.0)
    probability = raised / lax.optimization_barrier(jnp.sum(raised, axis=-1, keepdims=True))
    rounded_prob = probability.astype(jnp.bfloat16)
    attended = jnp.einsum('hts,shd->thd', rounded_prob.astype(jnp.float32), values_shared).astype(jnp.bfloat16)
    attended_flat = attended.reshape(length, HEADS * HD)
    grad_attended = jnp.dot(upstream, out_weight.T, preferred_element_type=jnp.float32).astype(jnp.bfloat16)
    part_w_out = jnp.dot(attended_flat.T, upstream, preferred_element_type=jnp.float32)
    grad_heads = grad_attended.reshape(length, HEADS, HD).astype(jnp.float32)
    row_delta = lax.optimization_barrier(jnp.sum(grad_heads * attended.astype(jnp.float32), axis=-1)).T
    grad_probs = jnp.einsum('thd,shd->hts', grad_heads, values_shared)
    grad_scores = (probability * (grad_probs - row_delta[:, :, None]) * (1.0 - squashed * squashed) * score_scale).astype(jnp.bfloat16)
    score_grad_float = grad_scores.astype(jnp.float32)
    grad_queries = unrotate(jnp.einsum('hts,shd->thd', score_grad_float, keys_shared), cosine, sine_table).astype(jnp.bfloat16).reshape(length, HEADS * HD)
    key_each = unrotate(jnp.einsum('hts,thd->shd', score_grad_float, queries_float), cosine, sine_table).astype(jnp.bfloat16)
    value_each = jnp.einsum('hts,thd->shd', rounded_prob.astype(jnp.float32), grad_heads).astype(jnp.bfloat16)
    part_w_query = jnp.dot(normed.T, grad_queries, preferred_element_type=jnp.float32)
    grad_normed = jnp.dot(grad_queries, query_weight.T, preferred_element_type=jnp.float32)
    part_w_key = jnp.zeros(key_weight.shape, jnp.float32)
    part_w_value = jnp.zeros(value_weight.shape, jnp.float32)
    for parity in range(2):
        key_part = key_each[:, parity::2, :].reshape(length, KV_HEADS * HD)
        value_part = value_each[:, parity::2, :].reshape(length, KV_HEADS * HD)
        part_w_key = part_w_key + jnp.dot(normed.T, key_part, preferred_element_type=jnp.float32)
        part_w_value = part_w_value + jnp.dot(normed.T, value_part, preferred_element_type=jnp.float32)
        grad_normed = grad_normed + jnp.dot(key_part, key_weight.T, preferred_element_type=jnp.float32)
        grad_normed = grad_normed + jnp.dot(value_part, value_weight.T, preferred_element_type=jnp.float32)
    scaled_grad = grad_normed * gain_row
    branch = reciprocal * (scaled_grad - unit_rows * lax.optimization_barrier(jnp.mean(scaled_grad * unit_rows, axis=-1, keepdims=True)))
    layer_grad = (upstream.astype(jnp.float32) + branch).astype(jnp.bfloat16)
    gain_part = lax.optimization_barrier(jnp.sum(grad_normed * unit_rows, axis=0))
    return (layer_grad, part_w_query, part_w_key, part_w_value, part_w_out, gain_part)

def reference(layer_inputs, out_grad, gain, w_query, w_key, w_value, w_out, doc_lengths, window_reach):
    totals = [[None, None, None, None, None] for layer_number in range(LAYERS)]
    input_rows = []
    for sequence in range(N_DP):
        first_row = sequence * SEQ_LEN
        upstream = out_grad[first_row:first_row + SEQ_LEN]
        for layer_number in reversed(range(LAYERS)):
            results = layer_backward(layer_inputs[layer_number, first_row:first_row + SEQ_LEN], upstream, gain[layer_number], w_query[layer_number], w_key[layer_number], w_value[layer_number], w_out[layer_number], doc_lengths[sequence], window_reach[layer_number])
            upstream = results[0]
            for member in range(4):
                rounded = lax.optimization_barrier(results[member + 1].astype(jnp.bfloat16)).astype(jnp.float32)
                if totals[layer_number][member] is None:
                    totals[layer_number][member] = rounded
                else:
                    totals[layer_number][member] = totals[layer_number][member] + rounded
            if totals[layer_number][4] is None:
                totals[layer_number][4] = results[5]
            else:
                totals[layer_number][4] = totals[layer_number][4] + results[5]
        input_rows.append(upstream)
    input_grad = jnp.concatenate(input_rows, axis=0)
    stacks = [jnp.stack([totals[layer_number][member] for layer_number in range(LAYERS)]) / N_DP for member in range(5)]
    return (input_grad, stacks[0], stacks[1], stacks[2], stacks[3], stacks[4])
```

```python
import functools
import math

import jax
import jax.numpy as jnp
import numpy as np
from jax import lax
from jax.experimental import pallas as pl
from jax.experimental.pallas import tpu as pltpu
from jax.sharding import PartitionSpec as P

D = 4608
HEADS = 32
HD = 128
SEQ_LEN = 384
LAYERS = 2


softcap = 50.0
epsilon = 1e-06


def swapped(x, axis, bit):
    return lax.ppermute(x, axis, [(i, i ^ 1 << bit) for i in range(lax.axis_size(axis))])


def rope_tables(length, head_width):
    half_width = head_width // 2
    frequencies = jnp.exp(
        -jnp.arange(half_width).astype(jnp.float32) * (2.0 * math.log(10000.0) / head_width)
    )
    angles = jnp.arange(length).astype(jnp.float32)[:, None] * frequencies[None, :]
    return (jnp.cos(angles)[:, None, :], jnp.sin(angles)[:, None, :])


def rotate(values, cosine, sine_table):
    half_width = values.shape[-1] // 2
    first_half = values[..., :half_width]
    second_half = values[..., half_width:]
    return jnp.concatenate(
        [
            first_half * cosine - second_half * sine_table,
            second_half * cosine + first_half * sine_table,
        ],
        axis=-1,
    )


def unrotate(values, cosine, sine_table):
    half_width = values.shape[-1] // 2
    first_half = values[..., :half_width]
    second_half = values[..., half_width:]
    return jnp.concatenate(
        [
            first_half * cosine + second_half * sine_table,
            second_half * cosine - first_half * sine_table,
        ],
        axis=-1,
    )


def allowed_pairs(lengths_row, reach, length):
    doc_ends = jnp.cumsum(lengths_row)
    places = jnp.arange(length, dtype=jnp.int32)
    document = jnp.sum((places[:, None] >= doc_ends[None, :]).astype(jnp.int32), axis=1)
    same_doc = document[:, None] == document[None, :]
    causal = places[None, :] <= places[:, None]
    in_window = places[:, None] - places[None, :] < reach
    return same_doc & causal & in_window


def join_halves(own_part, other_part, parity):
    return jnp.where(
        parity == 0,
        jnp.concatenate([own_part, other_part], axis=-1),
        jnp.concatenate([other_part, own_part], axis=-1),
    )


def split_halves(matrix, parity):
    half_width = matrix.shape[-1] // 2
    lower_part = matrix[..., :half_width]
    upper_part = matrix[..., half_width:]
    return (
        jnp.where(parity == 0, lower_part, upper_part),
        jnp.where(parity == 0, upper_part, lower_part),
    )


def contract_rows(left_side, right_side):
    return lax.dot_general(
        left_side, right_side, (((0,), (0,)), ((), ())), preferred_element_type=jnp.float32
    )


def contract_cols(left_side, right_side):
    return lax.dot_general(
        left_side, right_side, (((1,), (1,)), ((), ())), preferred_element_type=jnp.float32
    )


def pair_stack(each_head, key_heads):
    length = each_head.shape[0]
    grouped = each_head.reshape(length, key_heads, 2, HD)
    return jnp.moveaxis(grouped, 2, 0).reshape(2, length, key_heads * HD)


def norm_backward(inputs, grad_normed, upstream, gain_row):
    matrix_rows = inputs.astype(jnp.float32)
    reciprocal = lax.rsqrt(jnp.mean(matrix_rows * matrix_rows, axis=-1, keepdims=True) + epsilon)
    unit_rows = matrix_rows * reciprocal
    scaled_grad = grad_normed * gain_row
    branch = reciprocal * (
        scaled_grad - unit_rows * jnp.mean(scaled_grad * unit_rows, axis=-1, keepdims=True)
    )
    layer_grad = (upstream.astype(jnp.float32) + branch).astype(jnp.bfloat16)
    return (layer_grad, grad_normed * unit_rows)


def local_general(layer_inputs, out_grad, gain, w_query, w_key, w_value, w_out, doc_lengths, window_reach):
    device_rank = lax.axis_index("tp")
    parity = device_rank % 2
    local_rows = SEQ_LEN // lax.axis_size("tp")
    query_heads = w_query.shape[2] // HD
    paired = query_heads == 1
    score_scale = (D // HEADS) ** (-0.5)
    cosine_table, sine_table = rope_tables(SEQ_LEN, HD)
    first_own = device_rank * local_rows
    full_upstream = out_grad
    grads_by_layer = [None] * LAYERS
    gain_terms = [None] * LAYERS
    for layer_number in reversed(range(LAYERS)):
        whole_inputs = layer_inputs[layer_number]
        gain_row = gain[layer_number]
        query_weight = w_query[layer_number]
        key_weight = w_key[layer_number]
        value_weight = w_value[layer_number]
        out_weight = w_out[layer_number]
        matrix_rows = whole_inputs.astype(jnp.float32)
        reciprocal = lax.rsqrt(
            jnp.mean(matrix_rows * matrix_rows, axis=-1, keepdims=True) + epsilon
        )
        normed = (matrix_rows * reciprocal * gain_row).astype(jnp.bfloat16)
        queries = rotate(
            jnp.dot(normed, query_weight, preferred_element_type=jnp.float32).reshape(
                SEQ_LEN, query_heads, HD
            ),
            cosine_table,
            sine_table,
        ).astype(jnp.bfloat16)
        if paired:
            partner_key, partner_value = swapped((key_weight, value_weight), "tp", 0)
            full_key_weight = join_halves(key_weight, partner_key, parity)
            full_value_weight = join_halves(value_weight, partner_value, parity)
            key_raw = jnp.dot(normed, full_key_weight, preferred_element_type=jnp.float32)
            value_raw = jnp.dot(normed, full_value_weight, preferred_element_type=jnp.float32)
            key_heads = 1
        else:
            key_raw = jnp.dot(normed, key_weight, preferred_element_type=jnp.float32)
            value_raw = jnp.dot(normed, value_weight, preferred_element_type=jnp.float32)
            key_heads = query_heads // 2
        keys_rope = rotate(
            key_raw.reshape(SEQ_LEN, key_heads, HD), cosine_table, sine_table
        ).astype(jnp.bfloat16)
        values_cast = value_raw.reshape(SEQ_LEN, key_heads, HD).astype(jnp.bfloat16)
        keys_shared = jnp.repeat(keys_rope, query_heads // key_heads, axis=1)
        values_shared = jnp.repeat(values_cast, query_heads // key_heads, axis=1)
        allowed = allowed_pairs(doc_lengths[0], window_reach[layer_number], SEQ_LEN)
        scores = (
            jnp.einsum("thd,shd->hts", queries, keys_shared, preferred_element_type=jnp.float32)
            * score_scale
        )
        squashed = jnp.tanh(scores / softcap)
        raised = jnp.where(allowed[None], jnp.exp(softcap * squashed), 0.0)
        probability = raised / jnp.sum(raised, axis=-1, keepdims=True)
        rounded_prob = probability.astype(jnp.bfloat16)
        attended = jnp.einsum(
            "hts,shd->thd", rounded_prob, values_shared, preferred_element_type=jnp.float32
        ).astype(jnp.bfloat16)
        attended_flat = attended.reshape(SEQ_LEN, query_heads * HD)
        grad_attended = contract_cols(full_upstream, out_weight).astype(jnp.bfloat16)
        grad_w_out = contract_rows(attended_flat, full_upstream)
        grad_heads = grad_attended.reshape(SEQ_LEN, query_heads, HD)
        row_delta = jnp.sum(
            grad_heads.astype(jnp.float32) * attended.astype(jnp.float32), axis=-1
        ).T
        grad_probs = jnp.einsum(
            "thd,shd->hts", grad_heads, values_shared, preferred_element_type=jnp.float32
        )
        grad_scores = (
            probability
            * (grad_probs - row_delta[:, :, None])
            * (1.0 - squashed * squashed)
            * score_scale
        ).astype(jnp.bfloat16)
        grad_queries = (
            unrotate(
                jnp.einsum(
                    "hts,shd->thd", grad_scores, keys_shared, preferred_element_type=jnp.float32
                ),
                cosine_table,
                sine_table,
            )
            .astype(jnp.bfloat16)
            .reshape(SEQ_LEN, query_heads * HD)
        )
        key_each = unrotate(
            jnp.einsum("hts,thd->shd", grad_scores, queries, preferred_element_type=jnp.float32),
            cosine_table,
            sine_table,
        ).astype(jnp.bfloat16)
        value_each = jnp.einsum(
            "hts,thd->shd", rounded_prob, grad_heads, preferred_element_type=jnp.float32
        ).astype(jnp.bfloat16)
        grad_w_query = contract_rows(normed, grad_queries)
        if paired:
            own_key_grad = key_each[:, 0, :]
            own_value_grad = value_each[:, 0, :]
            whole_key_grad = contract_rows(normed, own_key_grad)
            whole_value_grad = contract_rows(normed, own_value_grad)
            kept_key, sent_key = split_halves(whole_key_grad, parity)
            kept_value, sent_value = split_halves(whole_value_grad, parity)
            partner_key_grad, partner_value_grad = (
                swapped(sent_key.astype(jnp.bfloat16), "tp", 0).astype(sent_key.dtype),
                swapped(sent_value.astype(jnp.bfloat16), "tp", 0).astype(sent_value.dtype),
            )
            grad_w_key = kept_key + partner_key_grad
            grad_w_value = kept_value + partner_value_grad
            pair_terms = (
                (own_key_grad[None], full_key_weight),
                (own_value_grad[None], full_value_weight),
            )
        else:
            key_stack = pair_stack(key_each, key_heads)
            value_stack = pair_stack(value_each, key_heads)
            grad_w_key = contract_rows(normed, key_stack[0]) + contract_rows(normed, key_stack[1])
            grad_w_value = contract_rows(normed, value_stack[0]) + contract_rows(
                normed, value_stack[1]
            )
            pair_terms = ((key_stack, key_weight), (value_stack, value_weight))
        totals = contract_cols(grad_queries, query_weight)
        for stacked, weight in pair_terms:
            for grad_member in range(stacked.shape[0]):
                totals = totals + contract_cols(stacked[grad_member], weight)
        whole_grad = lax.psum(totals.astype(jnp.bfloat16), "tp").astype(jnp.float32)
        full_upstream, gain_rows = norm_backward(whole_inputs, whole_grad, full_upstream, gain_row)
        gain_terms[layer_number] = jnp.sum(
            lax.dynamic_slice_in_dim(gain_rows, first_own, local_rows, 0), axis=0
        )
        layer_grads = (grad_w_query, grad_w_key, grad_w_value, grad_w_out)
        grads_by_layer[layer_number] = layer_grads
    stacks = [
        jnp.stack([grads_by_layer[layer_number][member] for layer_number in range(LAYERS)])
        for member in range(4)
    ]
    stacks = (
        lax.psum_scatter(
            stacks[0].astype(jnp.bfloat16), "dp", scatter_dimension=1, tiled=True
        ).astype(jnp.float32),
        lax.psum_scatter(
            stacks[1].astype(jnp.bfloat16), "dp", scatter_dimension=1, tiled=True
        ).astype(jnp.float32),
        lax.psum_scatter(
            stacks[2].astype(jnp.bfloat16), "dp", scatter_dimension=1, tiled=True
        ).astype(jnp.float32),
        lax.psum_scatter(
            stacks[3].astype(jnp.bfloat16), "dp", scatter_dimension=2, tiled=True
        ).astype(jnp.float32),
    )
    group_count = lax.axis_size("dp")
    gain_total = lax.psum(jnp.stack(gain_terms), ("dp", "tp"))
    return (
        full_upstream,
        stacks[0] / group_count,
        stacks[1] / group_count,
        stacks[2] / group_count,
        stacks[3] / group_count,
        gain_total / group_count,
    )


def rope_wide(length, head_width):
    half_width = head_width // 2
    frequencies = np.exp(-np.arange(half_width) * (2.0 * math.log(10000.0) / head_width))
    angles = np.arange(length)[:, None] * frequencies[None, :]
    cosine, sine_table = (np.cos(angles), np.sin(angles))
    return (
        jnp.asarray(np.concatenate([cosine, cosine], axis=-1), jnp.float32),
        jnp.asarray(np.concatenate([-sine_table, sine_table], axis=-1), jnp.float32),
    )


def dot_nt(left_side, right_side):
    return lax.dot_general(
        left_side, right_side, (((1,), (1,)), ((), ())), preferred_element_type=jnp.float32
    )


def dot_nn(left_side, right_side):
    return lax.dot_general(
        left_side, right_side, (((1,), (0,)), ((), ())), preferred_element_type=jnp.float32
    )


def forward_kernel(
    layer, scale, rank, lengths, reach, x_ref, gain_ref, wq_ref, wk_ref, wv_ref, cos_ref, sin_ref,
    *rest,
):
    normed_refs = rest[: -10]
    q_ref, k_ref, v_ref, att_ref, prob_ref, slope_ref, recip_ref, accq, acck, accv = rest[-10:]
    step = pl.program_id(0)
    length = x_ref.shape[1]
    width = wq_ref.shape[1]
    row_block = 128

    @pl.when(step == 0)
    def _():
        x = x_ref[0].astype(jnp.float32)
        mean = jnp.mean(x * x, axis=-1, keepdims=True)
        recip_ref[...] = jnp.broadcast_to(lax.rsqrt(mean + epsilon), recip_ref.shape)
        accq[...] = jnp.zeros_like(accq)
        acck[...] = jnp.zeros_like(acck)
        accv[...] = jnp.zeros_like(accv)

    columns = pl.ds(pl.multiple_of((step ^ rank[0]) * width, 128), width)
    x = x_ref[0, :, columns].astype(jnp.float32)
    normed = (x * recip_ref[:, :1] * gain_ref[layer : layer + 1, columns]).astype(jnp.bfloat16)
    for mask, normed_ref in enumerate(normed_refs):

        @pl.when(step == mask)
        def _():
            normed_ref[...] = normed

    accq[...] += dot_nn(normed, wq_ref[0])
    acck[...] += dot_nn(normed, wk_ref[0])
    accv[...] += dot_nn(normed, wv_ref[0])

    @pl.when(step == pl.num_programs(0) - 1)
    def _():
        cosine, sine = (cos_ref[...], sin_ref[...])

        def turn(part):
            return part * cosine + pltpu.roll(part, HD // 2, 1) * sine

        v_ref[...] = accv[...].astype(jnp.bfloat16)
        for head in range(acck.shape[1] // HD):
            part = slice(head * HD, (head + 1) * HD)
            k_ref[:, part] = turn(acck[:, part]).astype(jnp.bfloat16)
        ends = [lengths[0, 0]]
        for doc in range(1, lengths.shape[1] - 1):
            ends.append(ends[-1] + lengths[0, doc])
        window = reach[layer]
        heads = accq.shape[1] // HD
        share = heads // (acck.shape[1] // HD)
        for head in range(heads):
            part = slice(head * HD, (head + 1) * HD)
            q_ref[:, part] = turn(accq[:, part]).astype(jnp.bfloat16)
        for block in range(length // row_block):
            rows = slice(block * row_block, (block + 1) * row_block)
            seen = (block + 1) * row_block
            row = block * row_block + lax.broadcasted_iota(jnp.int32, (row_block, seen), 0)
            col = lax.broadcasted_iota(jnp.int32, (row_block, seen), 1)
            first = row - window + 1
            for end in ends:
                first = jnp.maximum(first, jnp.where(row >= end, end, 0))
            allowed = (col <= row) & (col >= first)
            for head in range(heads):
                part = slice(head * HD, (head + 1) * HD)
                kv = head // share
                kv_part = slice(kv * HD, (kv + 1) * HD)
                scores = dot_nt(q_ref[rows, part], k_ref[:seen, kv_part]) * scale
                squashed = jnp.tanh(scores / softcap)
                raised = jnp.where(allowed, jnp.exp(softcap * squashed), 0.0)
                total = jnp.sum(raised, axis=-1, keepdims=True)
                probability = raised * (1.0 / total)
                rounded = probability.astype(jnp.bfloat16)
                prob_ref[head, rows, :seen] = rounded
                slope_ref[head, rows, :seen] = probability * ((1.0 - squashed * squashed) * scale)
                att_ref[rows, part] = dot_nn(rounded, v_ref[:seen, kv_part]).astype(jnp.bfloat16)


def forward_call(layer, steps, rank, layer_inputs, gain, w_query, w_key, w_value, lengths, reach, cosine, sine):
    _, length, depth = layer_inputs.shape
    width = depth // steps
    q_width, k_width = (w_query.shape[2], w_key.shape[2])
    heads = q_width // HD
    scale = (D // HEADS) ** (-0.5)
    smem = pl.BlockSpec(memory_space=pltpu.SMEM)

    def weight(columns):
        return pl.BlockSpec((1, width, columns), lambda k, rank: (layer, k ^ rank[0], 0))

    def whole(*shape):
        return pl.BlockSpec(shape, lambda k, rank: (0,) * len(shape))

    bf, f32 = (jnp.bfloat16, jnp.float32)
    shapes = [((length, width), bf)] * steps + [
        ((length, q_width), bf),
        ((length, k_width), bf),
        ((length, k_width), bf),
        ((length, q_width), bf),
        ((heads, length, length), bf),
        ((heads, length, length), f32),
        ((length, HD), f32),
    ]
    flops = 2 * length * depth * (q_width + 2 * k_width)
    return pl.pallas_call(
        functools.partial(forward_kernel, layer, scale),
        grid_spec=pltpu.PrefetchScalarGridSpec(
            num_scalar_prefetch=1,
            grid=(steps,),
            in_specs=[
                smem,
                smem,
                pl.BlockSpec((1, length, depth), lambda k, rank: (layer, 0, 0)),
                whole(*gain.shape),
                weight(q_width),
                weight(k_width),
                weight(k_width),
                whole(length, HD),
                whole(length, HD),
            ],
            out_specs=[whole(*shape) for shape, _ in shapes],
            scratch_shapes=[
                pltpu.VMEM((length, q_width), f32),
                pltpu.VMEM((length, k_width), f32),
                pltpu.VMEM((length, k_width), f32),
            ],
        ),
        out_shape=[jax.ShapeDtypeStruct(shape, kind) for shape, kind in shapes],
        cost_estimate=pl.CostEstimate(
            flops=flops, transcendentals=heads * length * length, bytes_accessed=20 << 20
        ),
    )(rank, lengths, reach, layer_inputs, gain, w_query, w_key, w_value, cosine, sine)


def attention_kernel(
    flat, chunks, side, rank, *refs,
):
    g_refs = refs[: 1 if flat else 4]
    wo_ref, q_ref, k_ref, v_ref, att_ref, prob_ref, slope_ref, cos_ref, sin_ref = refs[
        len(g_refs) : len(g_refs) + 9
    ]
    wq_ref, wk_ref, wv_ref, factor_ref, *rest = refs[len(g_refs) + 9 :]
    pieces = rest[2 * chunks : -4]
    acc, heads_ref, dk, dv = rest[-4:]
    others, owns = (rest[:chunks], rest[chunks : 2 * chunks])
    step = pl.program_id(0)
    steps = pl.num_programs(0) // 2
    length, q_width = acc.shape
    k_width = dk.shape[1]
    row_block = 128

    @pl.when(step == 0)
    def _():
        acc[...] = jnp.zeros_like(acc)

    if flat:

        @pl.when(step < steps)
        def _():
            acc[...] += dot_nt(g_refs[0][...], wo_ref[0])

        for mask, piece in enumerate(pieces):

            @pl.when(step == mask)
            def _():
                piece[...] = g_refs[0][...]

    else:
        for mask, g_ref in enumerate(g_refs):

            @pl.when(step == mask)
            def _():
                acc[...] += dot_nt(g_ref[...], wo_ref[0])

    @pl.when(step == steps - 1)
    def _():
        cosine, sine = (cos_ref[...], sin_ref[...])

        def unturn(part, rows):
            return part * cosine[rows] - pltpu.roll(part, HD // 2, 1) * sine[rows]

        heads_ref[...] = acc[...].astype(jnp.bfloat16)
        dk[...] = jnp.zeros_like(dk)
        dv[...] = jnp.zeros_like(dv)
        heads = q_width // HD
        share = heads // (k_width // HD)
        for head in range(heads):
            part = slice(head * HD, (head + 1) * HD)
            kv = head // share
            kv_part = slice(kv * HD, (kv + 1) * HD)
            for block in range(length // row_block):
                rows = slice(block * row_block, (block + 1) * row_block)
                seen = (block + 1) * row_block
                ga = heads_ref[rows, part]
                delta = jnp.sum(
                    ga.astype(jnp.float32) * att_ref[rows, part].astype(jnp.float32),
                    axis=-1,
                    keepdims=True,
                )
                grad_probs = dot_nt(ga, v_ref[:seen, kv_part])
                grad_scores = (slope_ref[head, rows, :seen] * (grad_probs - delta)).astype(
                    jnp.bfloat16
                )
                gq = dot_nn(grad_scores, k_ref[:seen, kv_part])
                factor_ref[rows, part] = unturn(gq, rows).astype(jnp.bfloat16)
                dk[:seen, kv_part] += contract_rows(grad_scores, q_ref[rows, part])
                dv[:seen, kv_part] += contract_rows(prob_ref[head, rows, :seen], ga)
        every = slice(0, length)
        for kv in range(k_width // HD):
            kv_part = slice(kv * HD, (kv + 1) * HD)
            factor_ref[:, q_width + kv * HD : q_width + (kv + 1) * HD] = unturn(
                dk[:, kv_part], every
            ).astype(jnp.bfloat16)
        factor_ref[:, q_width + k_width : q_width + 2 * k_width] = dv[...].astype(jnp.bfloat16)
        factor_ref[:, q_width + 2 * k_width :] = att_ref[...]

    @pl.when(step >= steps)
    def _():
        total = dot_nt(factor_ref[:, :q_width], wq_ref[0])
        total += dot_nt(factor_ref[:, q_width : q_width + k_width], wk_ref[0])
        total += dot_nt(factor_ref[:, q_width + k_width : q_width + 2 * k_width], wv_ref[0])
        rows = length // chunks

        @pl.when(step < steps + steps // 2)
        def _():
            for chunk in range(chunks):
                others[chunk][0] = total[chunk * rows : (chunk + 1) * rows].astype(jnp.bfloat16)

        @pl.when(step >= steps + steps // 2)
        def _():
            for chunk in range(chunks):
                owns[chunk][0] = total[chunk * rows : (chunk + 1) * rows].astype(jnp.bfloat16)


def attention_call(layer, steps, chunks, side, rank, upstream, w_out, forward, cosine, sine, w_query, w_key, w_value):
    q, k, v, att, prob, slope = forward[steps:-1]
    length, q_width = q.shape
    k_width = k.shape[1]
    depth = w_out.shape[2]
    width = depth // steps
    flat = len(upstream) == 1

    half = steps // 2

    def whole(*shape):
        return pl.BlockSpec(shape, lambda k, side, rank: (0,) * len(shape))

    def first(k):
        return jnp.minimum(k, steps - 1)

    def last(k, side):
        turn = jnp.maximum(k - steps, 0)
        block = turn + half * (1 - side[0])
        return jnp.where(block >= steps, block - steps, block)

    def weight(columns):
        return pl.BlockSpec((1, width, columns), lambda k, side, rank: (layer, last(k, side), 0))

    if flat:
        g_specs = [pl.BlockSpec((length, width), lambda k, side, rank: (0, first(k) ^ rank[0]))]
    else:
        g_specs = [whole(length, width)] * steps
    pieces = steps if flat else 0
    rows = length // chunks
    other_spec = pl.BlockSpec(
        (1, rows, width), lambda k, side, rank: (jnp.clip(k - steps, 0, half - 1), 0, 0)
    )
    own_spec = pl.BlockSpec(
        (1, rows, width), lambda k, side, rank: (jnp.clip(k - steps - half, 0, half - 1), 0, 0)
    )
    bf, f32 = (jnp.bfloat16, jnp.float32)
    f_width = 2 * (q_width + k_width)
    return pl.pallas_call(
        functools.partial(attention_kernel, flat, chunks),
        grid_spec=pltpu.PrefetchScalarGridSpec(
        num_scalar_prefetch=2,
        grid=(2 * steps,),
        in_specs=g_specs
        + [
            pl.BlockSpec((1, q_width, width), lambda k, side, rank: (layer, 0, first(k) ^ rank[0])),
            whole(*q.shape),
            whole(*k.shape),
            whole(*v.shape),
            whole(*att.shape),
            whole(*prob.shape),
            whole(*slope.shape),
            whole(length, HD),
            whole(length, HD),
            weight(q_width),
            weight(k_width),
            weight(k_width),
        ],
        out_specs=[
            whole(length, f_width),
        ]
        + [other_spec] * chunks
        + [own_spec] * chunks
        + [whole(length, width)] * pieces,
        scratch_shapes=[
            pltpu.VMEM((length, q_width), f32),
            pltpu.VMEM((length, q_width), bf),
            pltpu.VMEM((length, k_width), f32),
            pltpu.VMEM((length, k_width), f32),
        ],
        ),
        out_shape=[jax.ShapeDtypeStruct((length, f_width), bf)]
        + [jax.ShapeDtypeStruct((half, rows, width), bf)] * (2 * chunks)
        + [jax.ShapeDtypeStruct((length, width), bf)] * pieces,
        cost_estimate=pl.CostEstimate(
            flops=4 * length * depth * (q_width + k_width), transcendentals=0, bytes_accessed=20 << 20
        ),
    )(side, rank, *upstream, w_out, q, k, v, att, prob, slope, cosine, sine, w_query, w_key, w_value)


def norm_kernel(layer, flat, keep, steps, side, rank, own_ref, other_ref, x_ref, recip_ref, *refs):
    pieces = 1 if flat else steps
    g_refs, gain_ref, rest = (refs[:pieces], refs[pieces], refs[pieces + 1 :])
    outs = rest[-(1 if keep else steps) - 1 : -1]
    gain_out = rest[-1]
    halves, _, width = own_ref.shape
    depth = steps * width
    recip = recip_ref[:, :1]

    @pl.when(pl.program_id(0) == 0)
    def _():
        if len(rest) > len(outs) + 1:
            gain_out[...] = rest[len(outs)][...]
        else:
            gain_out[...] = jnp.zeros_like(gain_out)

    def grad_of(block):
        own, other = (own_ref[block % halves], other_ref[block % halves])
        pick = block // halves == side[0]
        return jnp.where(pick, own.astype(jnp.float32), other.astype(jnp.float32))

    total = jnp.zeros_like(recip)
    for mask in range(steps):
        block = mask ^ rank[0]
        columns = pl.ds(pl.multiple_of(block * width, 128), width)
        unit = x_ref[0, :, columns].astype(jnp.float32) * recip
        product = grad_of(block) * unit
        gain_out[:, columns] += jnp.sum(product.reshape(-1, 8, width), axis=0)
        total += jnp.sum(product * gain_ref[layer : layer + 1, columns], axis=-1, keepdims=True)
    mean = total / depth
    for mask in range(steps):
        block = mask ^ rank[0]
        columns = pl.ds(pl.multiple_of(block * width, 128), width)
        unit = x_ref[0, :, columns].astype(jnp.float32) * recip
        grad = grad_of(block) * gain_ref[layer : layer + 1, columns]
        g = (g_refs[0][:, columns] if flat else g_refs[mask][...]).astype(jnp.float32)
        value = (g + recip * (grad - unit * mean)).astype(jnp.bfloat16)
        if keep:
            outs[0][:, columns] = value
        else:
            outs[mask][...] = value


def norm_call(layer, chunk, side, rank, own, other, layer_inputs, recip, upstream, gain, keep, earlier):
    halves, rows, width = own.shape
    steps = 2 * halves
    length, depth = layer_inputs.shape[1:]
    flat = len(upstream) == 1
    parts = 3
    tile = rows // parts
    half_spec = pl.BlockSpec((halves, tile, width), lambda r: (0, r, 0))
    flat_spec = pl.BlockSpec((tile, depth), lambda r: (chunk * parts + r, 0))
    piece_spec = pl.BlockSpec((tile, width), lambda r: (chunk * parts + r, 0))
    gain_spec = pl.BlockSpec((8, depth), lambda r: (0, 0))
    smem = pl.BlockSpec(memory_space=pltpu.SMEM)
    extra = [] if earlier is None else list(earlier)
    outs = 1 if keep else steps
    first = 7 + len(upstream)
    return pl.pallas_call(
        functools.partial(norm_kernel, layer, flat, keep, steps),
        grid=(parts,),
        in_specs=[
            smem,
            smem,
            half_spec,
            half_spec,
            pl.BlockSpec((1, tile, depth), lambda r: (layer, chunk * parts + r, 0)),
            pl.BlockSpec((tile, HD), lambda r: (chunk * parts + r, 0)),
        ]
        + [flat_spec if flat else piece_spec] * len(upstream)
        + [pl.BlockSpec(gain.shape, lambda r: (0, 0))]
        + ([pl.BlockSpec(memory_space=pl.ANY)] * outs + [gain_spec])[: len(extra)],
        out_specs=[flat_spec if keep else piece_spec] * outs + [gain_spec],
        out_shape=[
            jax.ShapeDtypeStruct((length, depth) if keep else (length, width), jnp.bfloat16)
        ]
        * outs
        + [jax.ShapeDtypeStruct((8, depth), jnp.float32)],
        input_output_aliases={first + i: i for i in range(outs)} if extra else {},
        cost_estimate=pl.CostEstimate(
            flops=30 * rows * depth, transcendentals=0, bytes_accessed=4 << 20
        ),
    )(side, rank, own, other, layer_inputs, recip, *upstream, gain, *extra)


def weights_kernel(count, groups, *refs):
    normed = refs[:count]
    upstream = refs[count : 2 * count]
    factors = refs[2 * count : 3 * count]
    wq_ref, wk_ref, wv_ref, wo_ref = refs[-4:]
    q_width, k_width = (wq_ref.shape[2], wk_ref.shape[2])
    widths = (q_width, k_width, k_width)
    start = 0
    for out_ref, width in zip((wq_ref, wk_ref, wv_ref), widths):
        total = 0.0
        for member in range(count):
            total += contract_rows(normed[member][...], factors[member][:, start : start + width])
        out_ref[0] = total / groups
        start += width
    total = 0.0
    for member in range(count):
        total += contract_rows(factors[member][:, start:], upstream[member][...])
    wo_ref[0] = total / groups


def weights_call(layer, layers, normed, upstream, factors, q_width, k_width, earlier):
    count = len(normed)
    length, width = normed[0].shape
    tile = width // 3
    piece = pl.BlockSpec((length, tile), lambda n: (0, n))
    factor = pl.BlockSpec(factors[0].shape, lambda n: (0, 0))
    any_spec = pl.BlockSpec(memory_space=pl.ANY)
    extra = [] if earlier is None else list(earlier)
    f32 = jnp.float32

    def tall(columns):
        return pl.BlockSpec((1, tile, columns), lambda n: (layer, n, 0))

    return pl.pallas_call(
        functools.partial(weights_kernel, count, count),
        grid=(width // tile,),
        in_specs=[piece] * (2 * count) + [factor] * count + [any_spec] * len(extra),
        out_specs=[
            tall(q_width),
            tall(k_width),
            tall(k_width),
            pl.BlockSpec((1, q_width, tile), lambda n: (layer, 0, n)),
        ],
        out_shape=[
            jax.ShapeDtypeStruct((layers, width, q_width), f32),
            jax.ShapeDtypeStruct((layers, width, k_width), f32),
            jax.ShapeDtypeStruct((layers, width, k_width), f32),
            jax.ShapeDtypeStruct((layers, q_width, width), f32),
        ],
        input_output_aliases={3 * count + i: i for i in range(len(extra))},
        cost_estimate=pl.CostEstimate(
            flops=4 * count * length * width * (q_width + k_width),
            transcendentals=0,
            bytes_accessed=24 << 20,
        ),
    )(*normed, *upstream, *factors, *extra)


def xor_send(x, axis, mask):
    return lax.ppermute(x, axis, [(i, i ^ mask) for i in range(lax.axis_size(axis))])


def spread_pieces(pieces):
    return [pieces[0]] + [
        xor_send(piece, "dp", mask)
        for mask, piece in enumerate(pieces)
        if mask
    ]


def share_factor(factor):
    beside = xor_send(factor, "dp", 1)
    across = xor_send(factor, "dp", 2)
    return [factor, beside, across, xor_send(across, "dp", 1)]


def along_line(x, pairs):
    return lax.ppermute(
        x, "tp", [(2 * a + side, 2 * b + side) for a, b in pairs for side in range(2)]
    )


def rounded_sum(left, right):
    return (left.astype(jnp.float32) + right.astype(jnp.float32)).astype(jnp.bfloat16)


def after(value, *earlier):
    return lax.optimization_barrier((value, *earlier))[0]


class Wave:
    def __init__(self, sent, kept, outer):
        self.outer = outer
        self.value = list(kept)
        self.moved = [xor_send(part, "tp", 1) for part in sent]
        self.last = None

    def tie(self, value):
        return value if self.last is None else after(value, self.last)

    def step(self, chunk, stage):
        value, moved = (self.value[chunk], self.tie(self.moved[chunk]))
        if stage == 3:
            value = jnp.where(self.outer, moved, value)
        else:
            value = rounded_sum(value, moved)
        self.value[chunk] = self.last = value
        if stage == 0:
            self.moved[chunk] = along_line(value, [(0, 1), (3, 2)])
        elif stage == 1:
            self.moved[chunk] = along_line(value, [(1, 2), (2, 1)])
        elif stage == 2:
            self.moved[chunk] = along_line(value, [(1, 0), (2, 3)])
        else:
            self.moved[chunk] = xor_send(value, "tp", 1)


def local(layer_inputs, out_grad, gain, w_query, w_key, w_value, w_out, doc_lengths, window_reach):
    if w_query.shape[2] == HD or lax.axis_size("dp") != 4 or lax.axis_size("tp") != 8:
        return local_general(
            layer_inputs, out_grad, gain, w_query, w_key, w_value, w_out, doc_lengths, window_reach
        )
    count = lax.axis_size("dp")
    rank = lax.axis_index("dp").astype(jnp.int32).reshape(1)
    chunks = 4
    layers = layer_inputs.shape[0]
    length = layer_inputs.shape[1]
    q_width, k_width = (w_query.shape[2], w_key.shape[2])
    cosine, sine = rope_wide(length, HD)
    forwards, normed = ([None] * layers, [None] * layers)
    place = lax.axis_index("tp")
    side = (place % 2).astype(jnp.int32).reshape(1)
    line = place // 2
    outer = (line == 0) | (line == 3)

    def forward(layer, inputs):
        result = forward_call(
            layer, count, rank, inputs, gain, w_query, w_key, w_value, doc_lengths, window_reach,
            cosine, sine,
        )
        forwards[layer] = result
        normed[layer] = spread_pieces(result[:count])
        return result[0]

    def weights(layer, factors, sent, earlier):
        return weights_call(
            layer, layers, normed[layer], sent, factors, q_width, k_width, earlier
        )

    upstream = [out_grad]
    waiting = None
    grads = None
    gains = [None] * layers
    top = layers - 1
    for layer in reversed(range(layers)):
        if layer == top:
            forward(top, layer_inputs)
        factor, *partial = attention_call(
            layer, count, chunks, side, rank, upstream, w_out, forwards[layer], cosine, sine, w_query,
            w_key, w_value,
        )
        factors = share_factor(factor)
        sent = spread_pieces(partial[2 * chunks :] or upstream)
        wave = Wave(partial[:chunks], partial[chunks : 2 * chunks], outer)
        if layer:
            wave.last = forward(layer - 1, after(layer_inputs, factor))
        if waiting is not None:
            grads = weights(waiting[0], waiting[1], [after(waiting[2][0], factor)] + waiting[2][1:], grads)
            wave.last = grads[1]
        result = None
        for slot in range(chunks + 5):
            for stage in range(5):
                chunk = slot - stage
                if not 0 <= chunk < chunks:
                    continue
                if stage < 4:
                    wave.step(chunk, stage)
                    continue
                result = norm_call(
                    layer, chunk, side, rank, wave.value[chunk], wave.tie(wave.moved[chunk]),
                    layer_inputs, forwards[layer][-1], upstream, gain, layer == 0, result,
                )
                wave.last = result[-1]
        *upstream, gain_part = result
        waiting = (layer, factors, sent)
        gain_row = jnp.sum(gain_part, axis=0, keepdims=True)
        beside = xor_send(gain_row, "dp", 1)
        across, corner = (xor_send(gain_row, "dp", 2), xor_send(gain_row, "dp", 3))
        gains[layer] = ((gain_row + beside) + (across + corner)) / count
    grads = weights(waiting[0], waiting[1], waiting[2], grads)
    return (upstream[0], *grads, jnp.concatenate(gains, axis=0))


def solution(mesh):
    in_specs = (
        P(None, "dp", None),
        P("dp", None),
        P(),
        P(None, None, "tp"),
        P(None, None, "tp"),
        P(None, None, "tp"),
        P(None, "tp", None),
        P("dp", None),
        P(),
    )
    out_specs = (
        P("dp", None),
        P(None, "dp", "tp"),
        P(None, "dp", "tp"),
        P(None, "dp", "tp"),
        P(None, "tp", "dp"),
        P(),
    )

    return jax.shard_map(local, mesh=mesh, in_specs=in_specs, out_specs=out_specs, check_vma=False)
```

```python
import functools
import math

import jax
import jax.numpy as jnp
import numpy as np
from jax import lax
from jax.experimental import pallas as pl
from jax.experimental.pallas import tpu as pltpu
from jax.sharding import PartitionSpec as P

D = 4608
HEADS = 32
HD = 128
SEQ_LEN = 384
LAYERS = 2


softcap = 50.0
epsilon = 1e-06


def swapped(x, axis, bit):
    return lax.ppermute(x, axis, [(i, i ^ 1 << bit) for i in range(lax.axis_size(axis))])


def rope_tables(length, head_width):
    half_width = head_width // 2
    frequencies = jnp.exp(
        -jnp.arange(half_width).astype(jnp.float32) * (2.0 * math.log(10000.0) / head_width)
    )
    angles = jnp.arange(length).astype(jnp.float32)[:, None] * frequencies[None, :]
    return (jnp.cos(angles)[:, None, :], jnp.sin(angles)[:, None, :])


def rotate(values, cosine, sine_table):
    half_width = values.shape[-1] // 2
    first_half = values[..., :half_width]
    second_half = values[..., half_width:]
    return jnp.concatenate(
        [
            first_half * cosine - second_half * sine_table,
            second_half * cosine + first_half * sine_table,
        ],
        axis=-1,
    )


def unrotate(values, cosine, sine_table):
    half_width = values.shape[-1] // 2
    first_half = values[..., :half_width]
    second_half = values[..., half_width:]
    return jnp.concatenate(
        [
            first_half * cosine + second_half * sine_table,
            second_half * cosine - first_half * sine_table,
        ],
        axis=-1,
    )


def allowed_pairs(lengths_row, reach, length):
    doc_ends = jnp.cumsum(lengths_row)
    places = jnp.arange(length, dtype=jnp.int32)
    document = jnp.sum((places[:, None] >= doc_ends[None, :]).astype(jnp.int32), axis=1)
    same_doc = document[:, None] == document[None, :]
    causal = places[None, :] <= places[:, None]
    in_window = places[:, None] - places[None, :] < reach
    return same_doc & causal & in_window


def join_halves(own_part, other_part, parity):
    return jnp.where(
        parity == 0,
        jnp.concatenate([own_part, other_part], axis=-1),
        jnp.concatenate([other_part, own_part], axis=-1),
    )


def split_halves(matrix, parity):
    half_width = matrix.shape[-1] // 2
    lower_part = matrix[..., :half_width]
    upper_part = matrix[..., half_width:]
    return (
        jnp.where(parity == 0, lower_part, upper_part),
        jnp.where(parity == 0, upper_part, lower_part),
    )


def contract_rows(left_side, right_side):
    return lax.dot_general(
        left_side, right_side, (((0,), (0,)), ((), ())), preferred_element_type=jnp.float32
    )


def contract_cols(left_side, right_side):
    return lax.dot_general(
        left_side, right_side, (((1,), (1,)), ((), ())), preferred_element_type=jnp.float32
    )


def pair_stack(each_head, key_heads):
    length = each_head.shape[0]
    grouped = each_head.reshape(length, key_heads, 2, HD)
    return jnp.moveaxis(grouped, 2, 0).reshape(2, length, key_heads * HD)


def norm_backward(inputs, grad_normed, upstream, gain_row):
    matrix_rows = inputs.astype(jnp.float32)
    reciprocal = lax.rsqrt(jnp.mean(matrix_rows * matrix_rows, axis=-1, keepdims=True) + epsilon)
    unit_rows = matrix_rows * reciprocal
    scaled_grad = grad_normed * gain_row
    branch = reciprocal * (
        scaled_grad - unit_rows * jnp.mean(scaled_grad * unit_rows, axis=-1, keepdims=True)
    )
    layer_grad = (upstream.astype(jnp.float32) + branch).astype(jnp.bfloat16)
    return (layer_grad, grad_normed * unit_rows)


def local_general(layer_inputs, out_grad, gain, w_query, w_key, w_value, w_out, doc_lengths, window_reach):
    device_rank = lax.axis_index("tp")
    parity = device_rank % 2
    local_rows = SEQ_LEN // lax.axis_size("tp")
    query_heads = w_query.shape[2] // HD
    paired = query_heads == 1
    score_scale = (D // HEADS) ** (-0.5)
    cosine_table, sine_table = rope_tables(SEQ_LEN, HD)
    first_own = device_rank * local_rows
    full_upstream = out_grad
    grads_by_layer = [None] * LAYERS
    gain_terms = [None] * LAYERS
    for layer_number in reversed(range(LAYERS)):
        whole_inputs = layer_inputs[layer_number]
        gain_row = gain[layer_number]
        query_weight = w_query[layer_number]
        key_weight = w_key[layer_number]
        value_weight = w_value[layer_number]
        out_weight = w_out[layer_number]
        matrix_rows = whole_inputs.astype(jnp.float32)
        reciprocal = lax.rsqrt(
            jnp.mean(matrix_rows * matrix_rows, axis=-1, keepdims=True) + epsilon
        )
        normed = (matrix_rows * reciprocal * gain_row).astype(jnp.bfloat16)
        queries = rotate(
            jnp.dot(normed, query_weight, preferred_element_type=jnp.float32).reshape(
                SEQ_LEN, query_heads, HD
            ),
            cosine_table,
            sine_table,
        ).astype(jnp.bfloat16)
        if paired:
            partner_key, partner_value = swapped((key_weight, value_weight), "tp", 0)
            full_key_weight = join_halves(key_weight, partner_key, parity)
            full_value_weight = join_halves(value_weight, partner_value, parity)
            key_raw = jnp.dot(normed, full_key_weight, preferred_element_type=jnp.float32)
            value_raw = jnp.dot(normed, full_value_weight, preferred_element_type=jnp.float32)
            key_heads = 1
        else:
            key_raw = jnp.dot(normed, key_weight, preferred_element_type=jnp.float32)
            value_raw = jnp.dot(normed, value_weight, preferred_element_type=jnp.float32)
            key_heads = query_heads // 2
        keys_rope = rotate(
            key_raw.reshape(SEQ_LEN, key_heads, HD), cosine_table, sine_table
        ).astype(jnp.bfloat16)
        values_cast = value_raw.reshape(SEQ_LEN, key_heads, HD).astype(jnp.bfloat16)
        keys_shared = jnp.repeat(keys_rope, query_heads // key_heads, axis=1)
        values_shared = jnp.repeat(values_cast, query_heads // key_heads, axis=1)
        allowed = allowed_pairs(doc_lengths[0], window_reach[layer_number], SEQ_LEN)
        scores = (
            jnp.einsum("thd,shd->hts", queries, keys_shared, preferred_element_type=jnp.float32)
            * score_scale
        )
        squashed = jnp.tanh(scores / softcap)
        raised = jnp.where(allowed[None], jnp.exp(softcap * squashed), 0.0)
        probability = raised / jnp.sum(raised, axis=-1, keepdims=True)
        rounded_prob = probability.astype(jnp.bfloat16)
        attended = jnp.einsum(
            "hts,shd->thd", rounded_prob, values_shared, preferred_element_type=jnp.float32
        ).astype(jnp.bfloat16)
        attended_flat = attended.reshape(SEQ_LEN, query_heads * HD)
        grad_attended = contract_cols(full_upstream, out_weight).astype(jnp.bfloat16)
        grad_w_out = contract_rows(attended_flat, full_upstream)
        grad_heads = grad_attended.reshape(SEQ_LEN, query_heads, HD)
        row_delta = jnp.sum(
            grad_heads.astype(jnp.float32) * attended.astype(jnp.float32), axis=-1
        ).T
        grad_probs = jnp.einsum(
            "thd,shd->hts", grad_heads, values_shared, preferred_element_type=jnp.float32
        )
        grad_scores = (
            probability
            * (grad_probs - row_delta[:, :, None])
            * (1.0 - squashed * squashed)
            * score_scale
        ).astype(jnp.bfloat16)
        grad_queries = (
            unrotate(
                jnp.einsum(
                    "hts,shd->thd", grad_scores, keys_shared, preferred_element_type=jnp.float32
                ),
                cosine_table,
                sine_table,
            )
            .astype(jnp.bfloat16)
            .reshape(SEQ_LEN, query_heads * HD)
        )
        key_each = unrotate(
            jnp.einsum("hts,thd->shd", grad_scores, queries, preferred_element_type=jnp.float32),
            cosine_table,
            sine_table,
        ).astype(jnp.bfloat16)
        value_each = jnp.einsum(
            "hts,thd->shd", rounded_prob, grad_heads, preferred_element_type=jnp.float32
        ).astype(jnp.bfloat16)
        grad_w_query = contract_rows(normed, grad_queries)
        if paired:
            own_key_grad = key_each[:, 0, :]
            own_value_grad = value_each[:, 0, :]
            whole_key_grad = contract_rows(normed, own_key_grad)
            whole_value_grad = contract_rows(normed, own_value_grad)
            kept_key, sent_key = split_halves(whole_key_grad, parity)
            kept_value, sent_value = split_halves(whole_value_grad, parity)
            partner_key_grad, partner_value_grad = (
                swapped(sent_key.astype(jnp.bfloat16), "tp", 0).astype(sent_key.dtype),
                swapped(sent_value.astype(jnp.bfloat16), "tp", 0).astype(sent_value.dtype),
            )
            grad_w_key = kept_key + partner_key_grad
            grad_w_value = kept_value + partner_value_grad
            pair_terms = (
                (own_key_grad[None], full_key_weight),
                (own_value_grad[None], full_value_weight),
            )
        else:
            key_stack = pair_stack(key_each, key_heads)
            value_stack = pair_stack(value_each, key_heads)
            grad_w_key = contract_rows(normed, key_stack[0]) + contract_rows(normed, key_stack[1])
            grad_w_value = contract_rows(normed, value_stack[0]) + contract_rows(
                normed, value_stack[1]
            )
            pair_terms = ((key_stack, key_weight), (value_stack, value_weight))
        totals = contract_cols(grad_queries, query_weight)
        for stacked, weight in pair_terms:
            for grad_member in range(stacked.shape[0]):
                totals = totals + contract_cols(stacked[grad_member], weight)
        whole_grad = lax.psum(totals.astype(jnp.bfloat16), "tp").astype(jnp.float32)
        full_upstream, gain_rows = norm_backward(whole_inputs, whole_grad, full_upstream, gain_row)
        gain_terms[layer_number] = jnp.sum(
            lax.dynamic_slice_in_dim(gain_rows, first_own, local_rows, 0), axis=0
        )
        layer_grads = (grad_w_query, grad_w_key, grad_w_value, grad_w_out)
        grads_by_layer[layer_number] = layer_grads
    stacks = [
        jnp.stack([grads_by_layer[layer_number][member] for layer_number in range(LAYERS)])
        for member in range(4)
    ]
    stacks = (
        lax.psum_scatter(
            stacks[0].astype(jnp.bfloat16), "dp", scatter_dimension=1, tiled=True
        ).astype(jnp.float32),
        lax.psum_scatter(
            stacks[1].astype(jnp.bfloat16), "dp", scatter_dimension=1, tiled=True
        ).astype(jnp.float32),
        lax.psum_scatter(
            stacks[2].astype(jnp.bfloat16), "dp", scatter_dimension=1, tiled=True
        ).astype(jnp.float32),
        lax.psum_scatter(
            stacks[3].astype(jnp.bfloat16), "dp", scatter_dimension=2, tiled=True
        ).astype(jnp.float32),
    )
    group_count = lax.axis_size("dp")
    gain_total = lax.psum(jnp.stack(gain_terms), ("dp", "tp"))
    return (
        full_upstream,
        stacks[0] / group_count,
        stacks[1] / group_count,
        stacks[2] / group_count,
        stacks[3] / group_count,
        gain_total / group_count,
    )


def rope_wide(length, head_width):
    half_width = head_width // 2
    frequencies = np.exp(-np.arange(half_width) * (2.0 * math.log(10000.0) / head_width))
    angles = np.arange(length)[:, None] * frequencies[None, :]
    return jnp.asarray(np.concatenate([np.cos(angles), np.sin(angles)], axis=-1), jnp.float32)


def rope_factors(table):
    flipped = pltpu.roll(table, HD // 2, 1)
    low = lax.broadcasted_iota(jnp.int32, table.shape, 1) < HD // 2
    return (jnp.where(low, table, flipped), jnp.where(low, -flipped, table))


def dot_nt(left_side, right_side):
    return lax.dot_general(
        left_side, right_side, (((1,), (1,)), ((), ())), preferred_element_type=jnp.float32
    )


def dot_nn(left_side, right_side):
    return lax.dot_general(
        left_side, right_side, (((1,), (0,)), ((), ())), preferred_element_type=jnp.float32
    )


def project_kernel(layer, depth, rank, x_ref, gain_ref, wq_ref, wk_ref, wv_ref, rope_ref, *rest):
    scaled_refs = rest[:-8]
    q_ref, k_ref, v_ref, recip_ref, accq, acck, accv, squares = rest[-8:]
    step = pl.program_id(0)
    width = wq_ref.shape[1]

    @pl.when(step == 0)
    def _():
        accq[...] = jnp.zeros_like(accq)
        acck[...] = jnp.zeros_like(acck)
        accv[...] = jnp.zeros_like(accv)
        squares[...] = jnp.zeros_like(squares)

    columns = pl.ds(pl.multiple_of((step ^ rank[0]) * width, 128), width)
    x = x_ref[0].astype(jnp.float32)
    scaled = (x * gain_ref[layer : layer + 1, columns]).astype(jnp.bfloat16)
    square = x * x
    total = squares[...]
    for start in range(0, width, HD):
        total += square[:, start : start + HD]
    squares[...] = total
    for mask, scaled_ref in enumerate(scaled_refs):

        @pl.when(step == mask)
        def _():
            scaled_ref[...] = scaled

    accq[...] += dot_nn(scaled, wq_ref[0])
    acck[...] += dot_nn(scaled, wk_ref[0])
    accv[...] += dot_nn(scaled, wv_ref[0])

    @pl.when(step == pl.num_programs(0) - 1)
    def _():
        mean = jnp.sum(squares[...], axis=-1, keepdims=True) / depth
        recip = lax.rsqrt(mean + epsilon)
        recip_ref[...] = jnp.broadcast_to(recip, recip_ref.shape)
        cosine, sine = rope_factors(rope_ref[...])
        cosine, sine = (cosine * recip, sine * recip)

        def turn(part):
            return part * cosine + pltpu.roll(part, HD // 2, 1) * sine

        v_ref[...] = (accv[...] * recip).astype(jnp.bfloat16)
        for out_ref, acc in ((q_ref, accq), (k_ref, acck)):
            for head in range(acc.shape[1] // HD):
                part = slice(head * HD, (head + 1) * HD)
                out_ref[:, part] = turn(acc[:, part]).astype(jnp.bfloat16)


def project_call(layer, steps, rank, layer_inputs, gain, w_query, w_key, w_value, rope):
    _, length, depth = layer_inputs.shape
    width = depth // steps
    q_width, k_width = (w_query.shape[2], w_key.shape[2])

    def weight(columns):
        return pl.BlockSpec((1, width, columns), lambda k, rank: (layer, k ^ rank[0], 0))

    def whole(*shape):
        return pl.BlockSpec(shape, lambda k, rank: (0,) * len(shape))

    bf, f32 = (jnp.bfloat16, jnp.float32)
    shapes = [((length, width), bf)] * steps + [
        ((length, q_width), bf),
        ((length, k_width), bf),
        ((length, k_width), bf),
        ((length, HD), f32),
    ]
    return pl.pallas_call(
        functools.partial(project_kernel, layer, depth),
        grid_spec=pltpu.PrefetchScalarGridSpec(
            num_scalar_prefetch=1,
            grid=(steps,),
            in_specs=[
                pl.BlockSpec((1, length, width), lambda k, rank: (layer, 0, k ^ rank[0])),
                whole(*gain.shape),
                weight(q_width),
                weight(k_width),
                weight(k_width),
                whole(length, HD),
            ],
            out_specs=[whole(*shape) for shape, _ in shapes],
            scratch_shapes=[
                pltpu.VMEM((length, q_width), f32),
                pltpu.VMEM((length, k_width), f32),
                pltpu.VMEM((length, k_width), f32),
                pltpu.VMEM((length, HD), f32),
            ],
        ),
        out_shape=[jax.ShapeDtypeStruct(shape, kind) for shape, kind in shapes],
        cost_estimate=pl.CostEstimate(
            flops=2 * length * depth * (q_width + 2 * k_width),
            transcendentals=0,
            bytes_accessed=17 << 20,
        ),
    )(rank, layer_inputs, gain, w_query, w_key, w_value, rope)


def allowed_block(lengths, window, first_row, rows, seen):
    ends = [lengths[0, 0]]
    for doc in range(1, lengths.shape[1] - 1):
        ends.append(ends[-1] + lengths[0, doc])
    row = first_row + lax.broadcasted_iota(jnp.int32, (rows, seen), 0)
    col = lax.broadcasted_iota(jnp.int32, (rows, seen), 1)
    first = row - window + 1
    for end in ends:
        first = jnp.maximum(first, jnp.where(row >= end, end, 0))
    return (col <= row) & (col >= first)


def weigh(q, k, allowed):
    scale = (D // HEADS) ** (-0.5)
    squashed = jnp.tanh(dot_nt(q, k) * (scale / softcap))
    raised = jnp.where(allowed, jnp.exp(softcap * squashed), 0.0)
    probability = raised * (1.0 / jnp.sum(raised, axis=-1, keepdims=True))
    return (
        probability.astype(jnp.bfloat16),
        probability * (scale - squashed * squashed * scale),
    )


ROW_BLOCK = 128
CHUNKS = 4


def attend_kernel(layer, lengths, reach, q_ref, k_ref, v_ref, att_ref, prob_ref, slope_ref):
    length = q_ref.shape[0]
    for start in range(0, length, ROW_BLOCK):
        rows, seen = (slice(start, start + ROW_BLOCK), start + ROW_BLOCK)
        allowed = allowed_block(lengths, reach[layer], start, ROW_BLOCK, seen)
        rounded, slope = weigh(q_ref[rows], k_ref[:seen], allowed)
        prob_ref[0, rows, :seen] = rounded
        slope_ref[0, rows, :seen] = slope
        att_ref[rows] = dot_nn(rounded, v_ref[:seen]).astype(jnp.bfloat16)


def attend_call(layer, lengths, reach, q, k, v):
    length, q_width = q.shape
    heads = q_width // HD
    share = heads // (k.shape[1] // HD)
    smem = pl.BlockSpec(memory_space=pltpu.SMEM)
    own = pl.BlockSpec((length, HD), lambda h: (0, h))
    shared = pl.BlockSpec((length, HD), lambda h: (0, h // share))
    square = pl.BlockSpec((1, length, length), lambda h: (h, 0, 0))
    return pl.pallas_call(
        functools.partial(attend_kernel, layer),
        grid=(heads,),
        in_specs=[smem, smem, own, shared, shared],
        out_specs=[own, square, square],
        out_shape=[
            jax.ShapeDtypeStruct((length, q_width), jnp.bfloat16),
            jax.ShapeDtypeStruct((heads, length, length), jnp.bfloat16),
            jax.ShapeDtypeStruct((heads, length, length), jnp.float32),
        ],
        cost_estimate=pl.CostEstimate(
            flops=4 * heads * length * length * HD,
            transcendentals=2 * heads * length * length,
            bytes_accessed=6 << 20,
        ),
    )(lengths, reach, q, k, v)


def attention_kernel(layer, flat, fused, chunks, side, rank, *refs):
    g_refs, refs = (refs[: 1 if flat else 4], refs[1 if flat else 4 :])
    wo_ref, q_ref, k_ref, v_ref, rope_ref, recip_ref, wq_ref, wk_ref, wv_ref, *refs = refs
    if fused:
        lengths, reach, *refs = refs
    else:
        att_ref, prob_ref, slope_ref, *refs = refs
    shared_ref, *rest = refs
    acc, heads_ref, factor_ref, dk, dv = rest[-5:]
    others, owns = (rest[:chunks], rest[chunks : 2 * chunks])
    pieces = rest[2 * chunks : -5]
    step = pl.program_id(0)
    steps = pl.num_programs(0) // 2
    length, q_width = acc.shape
    k_width = dk.shape[1]

    @pl.when(step == 0)
    def _():
        acc[...] = jnp.zeros_like(acc)

    if flat:

        @pl.when(step < steps)
        def _():
            acc[...] += dot_nt(g_refs[0][...], wo_ref[0])

        for mask, piece in enumerate(pieces):

            @pl.when(step == mask)
            def _():
                piece[...] = g_refs[0][...]

    else:
        for mask, g_ref in enumerate(g_refs):

            @pl.when(step == mask)
            def _():
                acc[...] += dot_nt(g_ref[...], wo_ref[0])

    @pl.when(step == steps - 1)
    def _():
        cosine, sine = rope_factors(rope_ref[...])
        recip = recip_ref[:, :1]

        def unturn(part, rows):
            return part * cosine[rows] - pltpu.roll(part, HD // 2, 1) * sine[rows]

        heads_ref[...] = acc[...].astype(jnp.bfloat16)
        dk[...] = jnp.zeros_like(dk)
        dv[...] = jnp.zeros_like(dv)
        heads = q_width // HD
        share = heads // (k_width // HD)

        def group_step(group, carry):
            kv_part = pl.ds(pl.multiple_of(group * HD, HD), HD)
            for member in range(share):
                head = group * share + member
                part = pl.ds(pl.multiple_of(head * HD, HD), HD)
                att_part = pl.ds(pl.multiple_of(q_width + 2 * k_width + head * HD, HD), HD)
                for start in range(0, length, ROW_BLOCK):
                    rows, seen = (slice(start, start + ROW_BLOCK), start + ROW_BLOCK)
                    ga = heads_ref[rows, part]
                    if fused:
                        allowed = allowed_block(lengths, reach[layer], start, ROW_BLOCK, seen)
                        rounded, slope = weigh(q_ref[rows, part], k_ref[:seen, kv_part], allowed)
                        att = dot_nn(rounded, v_ref[:seen, kv_part]).astype(jnp.bfloat16)
                    else:
                        rounded = prob_ref[head, rows, :seen]
                        slope = slope_ref[head, rows, :seen]
                        att = att_ref[rows, part]
                    shared_ref[rows, att_part] = att
                    delta = jnp.sum(
                        ga.astype(jnp.float32) * att.astype(jnp.float32), axis=-1, keepdims=True
                    )
                    grad_probs = dot_nt(ga, v_ref[:seen, kv_part])
                    grad_scores = (slope * (grad_probs - delta)).astype(jnp.bfloat16)
                    gq = unturn(dot_nn(grad_scores, k_ref[:seen, kv_part]), rows)
                    factor_ref[rows, part] = gq.astype(jnp.bfloat16)
                    shared_ref[rows, part] = (gq * recip[rows]).astype(jnp.bfloat16)
                    dk[:seen, kv_part] += contract_rows(grad_scores, q_ref[rows, part])
                    dv[:seen, kv_part] += contract_rows(rounded, ga)
            return carry

        lax.fori_loop(0, k_width // HD, group_step, 0)
        every = slice(0, length)
        for kv in range(k_width // HD):
            kv_part = slice(kv * HD, (kv + 1) * HD)
            part = slice(q_width + kv * HD, q_width + (kv + 1) * HD)
            gk = unturn(dk[:, kv_part], every)
            factor_ref[:, part] = gk.astype(jnp.bfloat16)
            shared_ref[:, part] = (gk * recip).astype(jnp.bfloat16)
        part = slice(q_width + k_width, q_width + 2 * k_width)
        factor_ref[:, part] = dv[...].astype(jnp.bfloat16)
        shared_ref[:, part] = (dv[...] * recip).astype(jnp.bfloat16)

    @pl.when(step >= steps)
    def _():
        rows = length // chunks
        width = wq_ref.shape[1]
        tile = width // 3

        def tile_step(turn, carry):
            here = pl.ds(pl.multiple_of(turn * tile, 128), tile)
            total = dot_nt(factor_ref[:, :q_width], wq_ref[0, here])
            total += dot_nt(factor_ref[:, q_width : q_width + k_width], wk_ref[0, here])
            total += dot_nt(
                factor_ref[:, q_width + k_width : q_width + 2 * k_width], wv_ref[0, here]
            )

            @pl.when(step < steps + steps // 2)
            def _():
                for chunk in range(chunks):
                    others[chunk][0, :, here] = total[chunk * rows : (chunk + 1) * rows].astype(
                        jnp.bfloat16
                    )

            @pl.when(step >= steps + steps // 2)
            def _():
                for chunk in range(chunks):
                    owns[chunk][0, :, here] = total[chunk * rows : (chunk + 1) * rows].astype(
                        jnp.bfloat16
                    )

            return carry

        lax.fori_loop(0, 3, tile_step, 0)


def attention_call(
    layer, steps, chunks, side, rank, upstream, w_out, q, k, v, rope, recip, w_query, w_key,
    w_value, lengths, reach, saved,
):
    length, q_width = q.shape
    k_width = k.shape[1]
    depth = w_out.shape[2]
    width = depth // steps
    flat = len(upstream) == 1
    fused = saved is None
    half = steps // 2

    def whole(*shape):
        return pl.BlockSpec(shape, lambda k, side, rank: (0,) * len(shape))

    def first(k):
        return jnp.minimum(k, steps - 1)

    def last(k, side):
        turn = jnp.maximum(k - steps, 0)
        block = turn + half * (1 - side[0])
        return jnp.where(block >= steps, block - steps, block)

    def weight(columns):
        return pl.BlockSpec((1, width, columns), lambda k, side, rank: (layer, last(k, side), 0))

    if flat:
        g_specs = [pl.BlockSpec((length, width), lambda k, side, rank: (0, first(k) ^ rank[0]))]
    else:
        g_specs = [whole(length, width)] * steps
    pieces = steps if flat else 0
    rows = length // chunks
    other_spec = pl.BlockSpec(
        (1, rows, width), lambda k, side, rank: (jnp.clip(k - steps, 0, half - 1), 0, 0)
    )
    own_spec = pl.BlockSpec(
        (1, rows, width), lambda k, side, rank: (jnp.clip(k - steps - half, 0, half - 1), 0, 0)
    )
    smem = pl.BlockSpec(memory_space=pltpu.SMEM)
    extra = [lengths, reach] if fused else list(saved)
    bf, f32 = (jnp.bfloat16, jnp.float32)
    f_width = 2 * (q_width + k_width)
    return pl.pallas_call(
        functools.partial(attention_kernel, layer, flat, fused, chunks),
        grid_spec=pltpu.PrefetchScalarGridSpec(
            num_scalar_prefetch=2,
            grid=(2 * steps,),
            in_specs=g_specs
            + [
                pl.BlockSpec(
                    (1, q_width, width), lambda k, side, rank: (layer, 0, first(k) ^ rank[0])
                ),
                whole(*q.shape),
                whole(*k.shape),
                whole(*v.shape),
                whole(length, HD),
                whole(length, HD),
                weight(q_width),
                weight(k_width),
                weight(k_width),
            ]
            + ([smem, smem] if fused else [whole(*part.shape) for part in extra]),
            out_specs=[whole(length, f_width)]
            + [other_spec] * chunks
            + [own_spec] * chunks
            + [whole(length, width)] * pieces,
            scratch_shapes=[
                pltpu.VMEM((length, q_width), f32),
                pltpu.VMEM((length, q_width), bf),
                pltpu.VMEM((length, q_width + 2 * k_width), bf),
                pltpu.VMEM((length, k_width), f32),
                pltpu.VMEM((length, k_width), f32),
            ],
        ),
        out_shape=[jax.ShapeDtypeStruct((length, f_width), bf)]
        + [jax.ShapeDtypeStruct((half, rows, width), bf)] * (2 * chunks)
        + [jax.ShapeDtypeStruct((length, width), bf)] * pieces,
        cost_estimate=pl.CostEstimate(
            flops=4 * length * depth * (q_width + k_width),
            transcendentals=0,
            bytes_accessed=20 << 20,
        ),
    )(side, rank, *upstream, w_out, q, k, v, rope, recip, w_query, w_key, w_value, *extra)


NORM_ROWS = 16


def norm_kernel(layer, flat, keep, steps, count, parts, side, rank, *refs):
    owns, others, refs = (refs[:count], refs[count : 2 * count], refs[2 * count :])
    x_ref, recip_ref, *refs = refs
    pieces = 1 if flat else steps
    g_refs, gain_ref, rest = (refs[:pieces], refs[pieces], refs[pieces + 1 :])
    outs = rest[-(1 if keep else steps) - 1 : -1]
    gain_out = rest[-1]
    halves, tile, width = owns[0].shape
    depth = steps * width
    step = pl.program_id(0)

    @pl.when(step == 0)
    def _():
        if len(rest) > len(outs) + 1:
            gain_out[...] = rest[len(outs)][...]
        else:
            gain_out[...] = jnp.zeros_like(gain_out)

    def row_step(own_ref, other_ref, turn, carry):
        rows = pl.ds(pl.multiple_of(turn * NORM_ROWS, NORM_ROWS), NORM_ROWS)
        recip = recip_ref[rows, :1]

        def grad_of(block):
            pick = jnp.broadcast_to(block // halves == side[0], (NORM_ROWS, width))
            half = block % halves
            return jnp.where(pick, own_ref[half, rows], other_ref[half, rows]).astype(jnp.float32)

        total = jnp.zeros((NORM_ROWS, HD), jnp.float32)
        for mask in range(steps):
            block = mask ^ rank[0]
            columns = pl.ds(pl.multiple_of(block * width, 128), width)
            product = grad_of(block) * x_ref[0, rows, columns].astype(jnp.float32) * recip
            gain_out[:, columns] += product[:8] + product[8:]
            weighted = product * gain_ref[layer : layer + 1, columns]
            for start in range(0, width, HD):
                total += weighted[:, start : start + HD]
        slope = recip * recip * (jnp.sum(total, axis=-1, keepdims=True) / depth)
        for mask in range(steps):
            block = mask ^ rank[0]
            columns = pl.ds(pl.multiple_of(block * width, 128), width)
            g = g_refs[0][rows, columns] if flat else g_refs[mask][rows]
            value = (
                g.astype(jnp.float32)
                + grad_of(block) * gain_ref[layer : layer + 1, columns] * recip
                - x_ref[0, rows, columns].astype(jnp.float32) * slope
            ).astype(jnp.bfloat16)
            if keep:
                outs[0][rows, columns] = value
            else:
                outs[mask][rows] = value
        return carry

    for member in range(count):

        @pl.when(step // parts == member)
        def _():
            lax.fori_loop(
                0,
                tile // NORM_ROWS,
                functools.partial(row_step, owns[member], others[member]),
                0,
            )


def norm_call(
    layer, first, side, rank, owns, others, layer_inputs, recip, upstream, gain, keep, earlier
):
    count = len(owns)
    halves, rows, width = owns[0].shape
    steps = 2 * halves
    length, depth = layer_inputs.shape[1:]
    flat = len(upstream) == 1
    tile = 32
    parts = rows // tile
    start = first * parts

    def half_spec(member):
        return pl.BlockSpec(
            (halves, tile, width), lambda r: (0, jnp.clip(r - member * parts, 0, parts - 1), 0)
        )

    flat_spec = pl.BlockSpec((tile, depth), lambda r: (start + r, 0))
    piece_spec = pl.BlockSpec((tile, width), lambda r: (start + r, 0))
    gain_spec = pl.BlockSpec((8, depth), lambda r: (0, 0))
    smem = pl.BlockSpec(memory_space=pltpu.SMEM)
    extra = [] if earlier is None else list(earlier)
    outs = 1 if keep else steps
    before = 5 + 2 * count + len(upstream)
    return pl.pallas_call(
        functools.partial(norm_kernel, layer, flat, keep, steps, count, parts),
        grid=(count * parts,),
        in_specs=[smem, smem]
        + [half_spec(member) for member in range(count)] * 2
        + [
            pl.BlockSpec((1, tile, depth), lambda r: (layer, start + r, 0)),
            pl.BlockSpec((tile, HD), lambda r: (start + r, 0)),
        ]
        + [flat_spec if flat else piece_spec] * len(upstream)
        + [pl.BlockSpec(gain.shape, lambda r: (0, 0))]
        + ([pl.BlockSpec(memory_space=pl.ANY)] * outs + [gain_spec])[: len(extra)],
        out_specs=[flat_spec if keep else piece_spec] * outs + [gain_spec],
        out_shape=[
            jax.ShapeDtypeStruct((length, depth) if keep else (length, width), jnp.bfloat16)
        ]
        * outs
        + [jax.ShapeDtypeStruct((8, depth), jnp.float32)],
        input_output_aliases={before + i: i for i in range(outs)} if extra else {},
        cost_estimate=pl.CostEstimate(
            flops=30 * count * rows * depth, transcendentals=0, bytes_accessed=4 * count << 20
        ),
    )(side, rank, *owns, *others, layer_inputs, recip, *upstream, gain, *extra)


def weights_kernel(count, groups, *refs):
    normed = refs[:count]
    upstream = refs[count : 2 * count]
    factors = refs[2 * count : 3 * count]
    wq_ref, wk_ref, wv_ref, wo_ref = refs[-4:]
    q_width, k_width = (wq_ref.shape[2], wk_ref.shape[2])
    widths = (q_width, k_width, k_width)
    start = 0
    for out_ref, width in zip((wq_ref, wk_ref, wv_ref), widths):
        total = 0.0
        for member in range(count):
            total += contract_rows(normed[member][...], factors[member][:, start : start + width])
        out_ref[0] = total / groups
        start += width
    total = 0.0
    for member in range(count):
        total += contract_rows(factors[member][:, start:], upstream[member][...])
    wo_ref[0] = total / groups


def weights_call(
    layer, layers, normed, upstream, factors, q_width, k_width, earlier, first_tile, tiles
):
    count = len(normed)
    length, width = normed[0].shape
    tile = width // 3
    piece = pl.BlockSpec((length, tile), lambda n: (0, n + first_tile))
    factor = pl.BlockSpec(factors[0].shape, lambda n: (0, 0))
    any_spec = pl.BlockSpec(memory_space=pl.ANY)
    extra = [] if earlier is None else list(earlier)
    f32 = jnp.float32

    def tall(columns):
        return pl.BlockSpec((1, tile, columns), lambda n: (layer, n + first_tile, 0))

    return pl.pallas_call(
        functools.partial(weights_kernel, count, count),
        grid=(tiles,),
        in_specs=[piece] * (2 * count) + [factor] * count + [any_spec] * len(extra),
        out_specs=[
            tall(q_width),
            tall(k_width),
            tall(k_width),
            pl.BlockSpec((1, q_width, tile), lambda n: (layer, 0, n + first_tile)),
        ],
        out_shape=[
            jax.ShapeDtypeStruct((layers, width, q_width), f32),
            jax.ShapeDtypeStruct((layers, width, k_width), f32),
            jax.ShapeDtypeStruct((layers, width, k_width), f32),
            jax.ShapeDtypeStruct((layers, q_width, width), f32),
        ],
        input_output_aliases={3 * count + i: i for i in range(len(extra))},
        cost_estimate=pl.CostEstimate(
            flops=4 * count * length * tile * tiles * (q_width + k_width),
            transcendentals=0,
            bytes_accessed=8 * tiles << 20,
        ),
    )(*normed, *upstream, *factors, *extra)


def xor_send(x, axis, mask):
    return lax.ppermute(x, axis, [(i, i ^ mask) for i in range(lax.axis_size(axis))])


def spread_pieces(pieces):
    return [pieces[0]] + [
        xor_send(piece, "dp", mask)
        for mask, piece in enumerate(pieces)
        if mask
    ]


def share_factor(factor):
    beside = xor_send(factor, "dp", 1)
    across = xor_send(factor, "dp", 2)
    return [beside, across]


def along_line(x, pairs):
    return lax.ppermute(
        x, "tp", [(2 * a + side, 2 * b + side) for a, b in pairs for side in range(2)]
    )


def rounded_sum(left, right):
    return (left.astype(jnp.float32) + right.astype(jnp.float32)).astype(jnp.bfloat16)


def after(value, *earlier):
    return lax.optimization_barrier((value, *earlier))[0]


def wave_order(chunks):
    order = []
    for slot in range(chunks + 3):
        order += [(stage, slot - stage) for stage in range(4) if 0 <= slot - stage < chunks]
    return order + [(4, 0), (4, chunks - 1)]


class Wave:
    def __init__(self, sent, kept, outer):
        self.outer = outer
        self.value = list(kept)
        self.moved = [xor_send(part, "tp", 1) for part in sent]
        self.last = None

    def tie(self, value):
        return value if self.last is None else after(value, self.last)

    def step(self, chunk, stage):
        value, moved = (self.value[chunk], self.tie(self.moved[chunk]))
        if stage == 3:
            value = jnp.where(self.outer, moved, value)
        else:
            value = rounded_sum(value, moved)
        self.value[chunk] = self.last = value
        if stage == 0:
            self.moved[chunk] = along_line(value, [(0, 1), (3, 2)])
        elif stage == 1:
            self.moved[chunk] = along_line(value, [(1, 2), (2, 1)])
        elif stage == 2:
            self.moved[chunk] = along_line(value, [(1, 0), (2, 3)])
        else:
            self.moved[chunk] = xor_send(value, "tp", 1)


def local(layer_inputs, out_grad, gain, w_query, w_key, w_value, w_out, doc_lengths, window_reach):
    if w_query.shape[2] == HD or lax.axis_size("dp") != 4 or lax.axis_size("tp") != 8:
        return local_general(
            layer_inputs, out_grad, gain, w_query, w_key, w_value, w_out, doc_lengths, window_reach
        )
    count = lax.axis_size("dp")
    rank = lax.axis_index("dp").astype(jnp.int32).reshape(1)
    chunks = CHUNKS
    layers = layer_inputs.shape[0]
    length = layer_inputs.shape[1]
    q_width, k_width = (w_query.shape[2], w_key.shape[2])
    rope = rope_wide(length, HD)
    normed = [None] * layers
    place = lax.axis_index("tp")
    side = (place % 2).astype(jnp.int32).reshape(1)
    line = place // 2
    outer = (line == 0) | (line == 3)

    grads = None
    gains = [None] * layers
    top = layers - 1
    waiting = None
    upstream = [out_grad]

    def project(layer, inputs):
        result = project_call(
            layer, count, rank, inputs, gain, w_query, w_key, w_value, rope
        )
        return (result[:count], result[count : count + 3], result[-1])

    def weights(layer, factors, sent, tie):
        sent = [after(sent[0], tie)] + sent[1:]
        return weights_call(
            layer, layers, normed[layer], sent, factors, q_width, k_width, grads, 0, 3
        )

    pieces, heads, recip = project(top, layer_inputs)
    normed[top] = spread_pieces(pieces)
    saved = None
    for layer in reversed(range(layers)):
        factor, *partial = attention_call(
            layer, count, chunks, side, rank, upstream, w_out, *heads, rope, recip, w_query,
            w_key, w_value, doc_lengths, window_reach, saved,
        )
        wave = Wave(partial[:chunks], partial[chunks : 2 * chunks], outer)
        owned = partial[2 * chunks :] or upstream
        if layer:
            wave.last = after(layer_inputs, factor)
            next_pieces, next_heads, next_recip = project(layer - 1, wave.last)
            wave.last = next_heads[0]
        if waiting is not None:
            grads = weights(*waiting, factor)
            wave.last = grads[1]
        result = None
        for stage, chunk in wave_order(chunks):
            if stage < 4:
                wave.step(chunk, stage)
            else:
                members = range(chunk, chunks - 1) if chunk < chunks - 1 else range(chunk, chunks)
                result = norm_call(
                    layer, chunk, side, rank, [wave.value[member] for member in members],
                    [wave.tie(wave.moved[member]) for member in members], layer_inputs, recip,
                    upstream, gain, layer == 0, result,
                )
                wave.last = result[-1]
            if (stage, chunk) == (0, 0):
                tied = owned
                if layer == top:
                    tied = [
                        after(piece, wave.last) if mask else piece
                        for mask, piece in enumerate(owned)
                    ]
                factors = [factor] + share_factor(after(factor, wave.last))
                sent = spread_pieces(tied)
            if layer and (stage, chunk) == (0, 1):
                tied = [
                    after(piece, wave.last) if mask else piece
                    for mask, piece in enumerate(next_pieces)
                ]
                normed[layer - 1] = spread_pieces(tied)
            if (stage, chunk) == (2, chunks - 1):
                factors.append(xor_send(after(factors[2], wave.last), "dp", 1))
            if (stage, chunk) == (3, chunks - 2):
                if layer:
                    saved = attend_call(
                        layer - 1, doc_lengths, window_reach, wave.tie(next_heads[0]),
                        *next_heads[1:],
                    )
                    wave.last = saved[0]
                else:
                    grads = weights(layer, factors, sent, wave.last)
                    wave.last = grads[1]
        *upstream, gain_part = result
        waiting = (layer, factors, sent)
        if layer:
            heads, recip = (next_heads, next_recip)
        gains[layer] = gain_part
    gain_rows = jnp.stack([jnp.sum(part, axis=0) for part in lax.optimization_barrier(gains)])
    beside, across, corner = (
        xor_send(gain_rows, "dp", mask) for mask in range(1, 4)
    )
    gain_total = ((gain_rows + beside) + (across + corner)) / count
    return (upstream[0], *grads, gain_total)


def solution(mesh):
    in_specs = (
        P(None, "dp", None),
        P("dp", None),
        P(),
        P(None, None, "tp"),
        P(None, None, "tp"),
        P(None, None, "tp"),
        P(None, "tp", None),
        P("dp", None),
        P(),
    )
    out_specs = (
        P("dp", None),
        P(None, "dp", "tp"),
        P(None, "dp", "tp"),
        P(None, "dp", "tp"),
        P(None, "tp", "dp"),
        P(),
    )

    return jax.shard_map(local, mesh=mesh, in_specs=in_specs, out_specs=out_specs, check_vma=False)
```

```python
import functools
import math

import jax
import jax.numpy as jnp
import numpy as np
from jax import lax
from jax.experimental import pallas as pl
from jax.experimental.pallas import tpu as pltpu
from jax.sharding import PartitionSpec as P

D = 4608
HEADS = 32
HD = 128
SEQ_LEN = 384
LAYERS = 2


softcap = 50.0
epsilon = 1e-06


def swapped(x, axis, bit):
    return lax.ppermute(x, axis, [(i, i ^ 1 << bit) for i in range(lax.axis_size(axis))])


def rope_tables(length, head_width):
    half_width = head_width // 2
    frequencies = jnp.exp(
        -jnp.arange(half_width).astype(jnp.float32) * (2.0 * math.log(10000.0) / head_width)
    )
    angles = jnp.arange(length).astype(jnp.float32)[:, None] * frequencies[None, :]
    return (jnp.cos(angles)[:, None, :], jnp.sin(angles)[:, None, :])


def rotate(values, cosine, sine_table):
    half_width = values.shape[-1] // 2
    first_half = values[..., :half_width]
    second_half = values[..., half_width:]
    return jnp.concatenate(
        [
            first_half * cosine - second_half * sine_table,
            second_half * cosine + first_half * sine_table,
        ],
        axis=-1,
    )


def unrotate(values, cosine, sine_table):
    half_width = values.shape[-1] // 2
    first_half = values[..., :half_width]
    second_half = values[..., half_width:]
    return jnp.concatenate(
        [
            first_half * cosine + second_half * sine_table,
            second_half * cosine - first_half * sine_table,
        ],
        axis=-1,
    )


def allowed_pairs(lengths_row, reach, length):
    doc_ends = jnp.cumsum(lengths_row)
    places = jnp.arange(length, dtype=jnp.int32)
    document = jnp.sum((places[:, None] >= doc_ends[None, :]).astype(jnp.int32), axis=1)
    same_doc = document[:, None] == document[None, :]
    causal = places[None, :] <= places[:, None]
    in_window = places[:, None] - places[None, :] < reach
    return same_doc & causal & in_window


def join_halves(own_part, other_part, parity):
    return jnp.where(
        parity == 0,
        jnp.concatenate([own_part, other_part], axis=-1),
        jnp.concatenate([other_part, own_part], axis=-1),
    )


def split_halves(matrix, parity):
    half_width = matrix.shape[-1] // 2
    lower_part = matrix[..., :half_width]
    upper_part = matrix[..., half_width:]
    return (
        jnp.where(parity == 0, lower_part, upper_part),
        jnp.where(parity == 0, upper_part, lower_part),
    )


def contract_rows(left_side, right_side):
    return lax.dot_general(
        left_side, right_side, (((0,), (0,)), ((), ())), preferred_element_type=jnp.float32
    )


def contract_cols(left_side, right_side):
    return lax.dot_general(
        left_side, right_side, (((1,), (1,)), ((), ())), preferred_element_type=jnp.float32
    )


def pair_stack(each_head, key_heads):
    length = each_head.shape[0]
    grouped = each_head.reshape(length, key_heads, 2, HD)
    return jnp.moveaxis(grouped, 2, 0).reshape(2, length, key_heads * HD)


def norm_backward(inputs, grad_normed, upstream, gain_row):
    matrix_rows = inputs.astype(jnp.float32)
    reciprocal = lax.rsqrt(jnp.mean(matrix_rows * matrix_rows, axis=-1, keepdims=True) + epsilon)
    unit_rows = matrix_rows * reciprocal
    scaled_grad = grad_normed * gain_row
    branch = reciprocal * (
        scaled_grad - unit_rows * jnp.mean(scaled_grad * unit_rows, axis=-1, keepdims=True)
    )
    layer_grad = (upstream.astype(jnp.float32) + branch).astype(jnp.bfloat16)
    return (layer_grad, grad_normed * unit_rows)


def local_general(layer_inputs, out_grad, gain, w_query, w_key, w_value, w_out, doc_lengths, window_reach):
    device_rank = lax.axis_index("tp")
    parity = device_rank % 2
    local_rows = SEQ_LEN // lax.axis_size("tp")
    query_heads = w_query.shape[2] // HD
    paired = query_heads == 1
    score_scale = (D // HEADS) ** (-0.5)
    cosine_table, sine_table = rope_tables(SEQ_LEN, HD)
    first_own = device_rank * local_rows
    full_upstream = out_grad
    grads_by_layer = [None] * LAYERS
    gain_terms = [None] * LAYERS
    for layer_number in reversed(range(LAYERS)):
        whole_inputs = layer_inputs[layer_number]
        gain_row = gain[layer_number]
        query_weight = w_query[layer_number]
        key_weight = w_key[layer_number]
        value_weight = w_value[layer_number]
        out_weight = w_out[layer_number]
        matrix_rows = whole_inputs.astype(jnp.float32)
        reciprocal = lax.rsqrt(
            jnp.mean(matrix_rows * matrix_rows, axis=-1, keepdims=True) + epsilon
        )
        normed = (matrix_rows * reciprocal * gain_row).astype(jnp.bfloat16)
        queries = rotate(
            jnp.dot(normed, query_weight, preferred_element_type=jnp.float32).reshape(
                SEQ_LEN, query_heads, HD
            ),
            cosine_table,
            sine_table,
        ).astype(jnp.bfloat16)
        if paired:
            partner_key, partner_value = swapped((key_weight, value_weight), "tp", 0)
            full_key_weight = join_halves(key_weight, partner_key, parity)
            full_value_weight = join_halves(value_weight, partner_value, parity)
            key_raw = jnp.dot(normed, full_key_weight, preferred_element_type=jnp.float32)
            value_raw = jnp.dot(normed, full_value_weight, preferred_element_type=jnp.float32)
            key_heads = 1
        else:
            key_raw = jnp.dot(normed, key_weight, preferred_element_type=jnp.float32)
            value_raw = jnp.dot(normed, value_weight, preferred_element_type=jnp.float32)
            key_heads = query_heads // 2
        keys_rope = rotate(
            key_raw.reshape(SEQ_LEN, key_heads, HD), cosine_table, sine_table
        ).astype(jnp.bfloat16)
        values_cast = value_raw.reshape(SEQ_LEN, key_heads, HD).astype(jnp.bfloat16)
        keys_shared = jnp.repeat(keys_rope, query_heads // key_heads, axis=1)
        values_shared = jnp.repeat(values_cast, query_heads // key_heads, axis=1)
        allowed = allowed_pairs(doc_lengths[0], window_reach[layer_number], SEQ_LEN)
        scores = (
            jnp.einsum("thd,shd->hts", queries, keys_shared, preferred_element_type=jnp.float32)
            * score_scale
        )
        squashed = jnp.tanh(scores / softcap)
        raised = jnp.where(allowed[None], jnp.exp(softcap * squashed), 0.0)
        probability = raised / jnp.sum(raised, axis=-1, keepdims=True)
        rounded_prob = probability.astype(jnp.bfloat16)
        attended = jnp.einsum(
            "hts,shd->thd", rounded_prob, values_shared, preferred_element_type=jnp.float32
        ).astype(jnp.bfloat16)
        attended_flat = attended.reshape(SEQ_LEN, query_heads * HD)
        grad_attended = contract_cols(full_upstream, out_weight).astype(jnp.bfloat16)
        grad_w_out = contract_rows(attended_flat, full_upstream)
        grad_heads = grad_attended.reshape(SEQ_LEN, query_heads, HD)
        row_delta = jnp.sum(
            grad_heads.astype(jnp.float32) * attended.astype(jnp.float32), axis=-1
        ).T
        grad_probs = jnp.einsum(
            "thd,shd->hts", grad_heads, values_shared, preferred_element_type=jnp.float32
        )
        grad_scores = (
            probability
            * (grad_probs - row_delta[:, :, None])
            * (1.0 - squashed * squashed)
            * score_scale
        ).astype(jnp.bfloat16)
        grad_queries = (
            unrotate(
                jnp.einsum(
                    "hts,shd->thd", grad_scores, keys_shared, preferred_element_type=jnp.float32
                ),
                cosine_table,
                sine_table,
            )
            .astype(jnp.bfloat16)
            .reshape(SEQ_LEN, query_heads * HD)
        )
        key_each = unrotate(
            jnp.einsum("hts,thd->shd", grad_scores, queries, preferred_element_type=jnp.float32),
            cosine_table,
            sine_table,
        ).astype(jnp.bfloat16)
        value_each = jnp.einsum(
            "hts,thd->shd", rounded_prob, grad_heads, preferred_element_type=jnp.float32
        ).astype(jnp.bfloat16)
        grad_w_query = contract_rows(normed, grad_queries)
        if paired:
            own_key_grad = key_each[:, 0, :]
            own_value_grad = value_each[:, 0, :]
            whole_key_grad = contract_rows(normed, own_key_grad)
            whole_value_grad = contract_rows(normed, own_value_grad)
            kept_key, sent_key = split_halves(whole_key_grad, parity)
            kept_value, sent_value = split_halves(whole_value_grad, parity)
            partner_key_grad, partner_value_grad = (
                swapped(sent_key.astype(jnp.bfloat16), "tp", 0).astype(sent_key.dtype),
                swapped(sent_value.astype(jnp.bfloat16), "tp", 0).astype(sent_value.dtype),
            )
            grad_w_key = kept_key + partner_key_grad
            grad_w_value = kept_value + partner_value_grad
            pair_terms = (
                (own_key_grad[None], full_key_weight),
                (own_value_grad[None], full_value_weight),
            )
        else:
            key_stack = pair_stack(key_each, key_heads)
            value_stack = pair_stack(value_each, key_heads)
            grad_w_key = contract_rows(normed, key_stack[0]) + contract_rows(normed, key_stack[1])
            grad_w_value = contract_rows(normed, value_stack[0]) + contract_rows(
                normed, value_stack[1]
            )
            pair_terms = ((key_stack, key_weight), (value_stack, value_weight))
        totals = contract_cols(grad_queries, query_weight)
        for stacked, weight in pair_terms:
            for grad_member in range(stacked.shape[0]):
                totals = totals + contract_cols(stacked[grad_member], weight)
        whole_grad = lax.psum(totals.astype(jnp.bfloat16), "tp").astype(jnp.float32)
        full_upstream, gain_rows = norm_backward(whole_inputs, whole_grad, full_upstream, gain_row)
        gain_terms[layer_number] = jnp.sum(
            lax.dynamic_slice_in_dim(gain_rows, first_own, local_rows, 0), axis=0
        )
        layer_grads = (grad_w_query, grad_w_key, grad_w_value, grad_w_out)
        grads_by_layer[layer_number] = layer_grads
    stacks = [
        jnp.stack([grads_by_layer[layer_number][member] for layer_number in range(LAYERS)])
        for member in range(4)
    ]
    stacks = (
        lax.psum_scatter(
            stacks[0].astype(jnp.bfloat16), "dp", scatter_dimension=1, tiled=True
        ).astype(jnp.float32),
        lax.psum_scatter(
            stacks[1].astype(jnp.bfloat16), "dp", scatter_dimension=1, tiled=True
        ).astype(jnp.float32),
        lax.psum_scatter(
            stacks[2].astype(jnp.bfloat16), "dp", scatter_dimension=1, tiled=True
        ).astype(jnp.float32),
        lax.psum_scatter(
            stacks[3].astype(jnp.bfloat16), "dp", scatter_dimension=2, tiled=True
        ).astype(jnp.float32),
    )
    group_count = lax.axis_size("dp")
    gain_total = lax.psum(jnp.stack(gain_terms), ("dp", "tp"))
    return (
        full_upstream,
        stacks[0] / group_count,
        stacks[1] / group_count,
        stacks[2] / group_count,
        stacks[3] / group_count,
        gain_total / group_count,
    )


def rope_wide(length, head_width):
    half_width = head_width // 2
    frequencies = np.exp(-np.arange(half_width) * (2.0 * math.log(10000.0) / head_width))
    angles = np.arange(length)[:, None] * frequencies[None, :]
    return jnp.asarray(np.concatenate([np.cos(angles), np.sin(angles)], axis=-1), jnp.float32)


def rope_factors(table):
    flipped = pltpu.roll(table, HD // 2, 1)
    low = lax.broadcasted_iota(jnp.int32, table.shape, 1) < HD // 2
    return (jnp.where(low, table, flipped), jnp.where(low, -flipped, table))


def dot_nt(left_side, right_side):
    return lax.dot_general(
        left_side, right_side, (((1,), (1,)), ((), ())), preferred_element_type=jnp.float32
    )


def dot_nn(left_side, right_side):
    return lax.dot_general(
        left_side, right_side, (((1,), (0,)), ((), ())), preferred_element_type=jnp.float32
    )


def project_kernel(layer, depth, rank, x_ref, gain_ref, wq_ref, wk_ref, wv_ref, rope_ref, *rest):
    scaled_refs = rest[:-8]
    q_ref, k_ref, v_ref, recip_ref, accq, acck, accv, squares = rest[-8:]
    step = pl.program_id(0)
    width = wq_ref.shape[1]

    @pl.when(step == 0)
    def _():
        accq[...] = jnp.zeros_like(accq)
        acck[...] = jnp.zeros_like(acck)
        accv[...] = jnp.zeros_like(accv)
        squares[...] = jnp.zeros_like(squares)

    columns = pl.ds(pl.multiple_of((step ^ rank[0]) * width, 128), width)
    x = x_ref[0].astype(jnp.float32)
    scaled = (x * gain_ref[layer : layer + 1, columns]).astype(jnp.bfloat16)
    square = x * x
    total = squares[...]
    for start in range(0, width, HD):
        total += square[:, start : start + HD]
    squares[...] = total
    for mask, scaled_ref in enumerate(scaled_refs):

        @pl.when(step == mask)
        def _():
            scaled_ref[...] = scaled

    accq[...] += dot_nn(scaled, wq_ref[0])
    acck[...] += dot_nn(scaled, wk_ref[0])
    accv[...] += dot_nn(scaled, wv_ref[0])

    @pl.when(step == pl.num_programs(0) - 1)
    def _():
        mean = jnp.sum(squares[...], axis=-1, keepdims=True) / depth
        recip = lax.rsqrt(mean + epsilon)
        recip_ref[...] = jnp.broadcast_to(recip, recip_ref.shape)
        cosine, sine = rope_factors(rope_ref[...])
        cosine, sine = (cosine * recip, sine * recip)

        def turn(part):
            return part * cosine + pltpu.roll(part, HD // 2, 1) * sine

        v_ref[...] = (accv[...] * recip).astype(jnp.bfloat16)
        for out_ref, acc in ((q_ref, accq), (k_ref, acck)):
            for head in range(acc.shape[1] // HD):
                part = slice(head * HD, (head + 1) * HD)
                out_ref[:, part] = turn(acc[:, part]).astype(jnp.bfloat16)


def project_call(layer, steps, rank, layer_inputs, gain, w_query, w_key, w_value, rope):
    _, length, depth = layer_inputs.shape
    width = depth // steps
    q_width, k_width = (w_query.shape[2], w_key.shape[2])

    def weight(columns):
        return pl.BlockSpec((1, width, columns), lambda k, rank: (layer, k ^ rank[0], 0))

    def whole(*shape):
        return pl.BlockSpec(shape, lambda k, rank: (0,) * len(shape))

    bf, f32 = (jnp.bfloat16, jnp.float32)
    shapes = [((length, width), bf)] * steps + [
        ((length, q_width), bf),
        ((length, k_width), bf),
        ((length, k_width), bf),
        ((length, HD), f32),
    ]
    return pl.pallas_call(
        functools.partial(project_kernel, layer, depth),
        grid_spec=pltpu.PrefetchScalarGridSpec(
            num_scalar_prefetch=1,
            grid=(steps,),
            in_specs=[
                pl.BlockSpec((1, length, width), lambda k, rank: (layer, 0, k ^ rank[0])),
                whole(*gain.shape),
                weight(q_width),
                weight(k_width),
                weight(k_width),
                whole(length, HD),
            ],
            out_specs=[whole(*shape) for shape, _ in shapes],
            scratch_shapes=[
                pltpu.VMEM((length, q_width), f32),
                pltpu.VMEM((length, k_width), f32),
                pltpu.VMEM((length, k_width), f32),
                pltpu.VMEM((length, HD), f32),
            ],
        ),
        out_shape=[jax.ShapeDtypeStruct(shape, kind) for shape, kind in shapes],
        cost_estimate=pl.CostEstimate(
            flops=2 * length * depth * (q_width + 2 * k_width),
            transcendentals=0,
            bytes_accessed=17 << 20,
        ),
    )(rank, layer_inputs, gain, w_query, w_key, w_value, rope)


def allowed_block(lengths, window, first_row, rows, seen):
    ends = [lengths[0, 0]]
    for doc in range(1, lengths.shape[1] - 1):
        ends.append(ends[-1] + lengths[0, doc])
    row = first_row + lax.broadcasted_iota(jnp.int32, (rows, seen), 0)
    col = lax.broadcasted_iota(jnp.int32, (rows, seen), 1)
    first = row - window + 1
    for end in ends:
        first = jnp.maximum(first, jnp.where(row >= end, end, 0))
    return (col <= row) & (col >= first)


def weigh(q, k, allowed):
    scale = (D // HEADS) ** (-0.5)
    squashed = jnp.tanh(dot_nt(q, k) * (scale / softcap))
    raised = jnp.where(allowed, jnp.exp(softcap * squashed), 0.0)
    probability = raised * (1.0 / jnp.sum(raised, axis=-1, keepdims=True))
    return (
        probability.astype(jnp.bfloat16),
        probability * (scale - squashed * squashed * scale),
    )


ROW_BLOCK = 128
CHUNKS = 4


def attend_kernel(layer, lengths, reach, q_ref, k_ref, v_ref, att_ref, prob_ref, slope_ref):
    length = q_ref.shape[0]
    for start in range(0, length, ROW_BLOCK):
        rows, seen = (slice(start, start + ROW_BLOCK), start + ROW_BLOCK)
        allowed = allowed_block(lengths, reach[layer], start, ROW_BLOCK, seen)
        rounded, slope = weigh(q_ref[rows], k_ref[:seen], allowed)
        prob_ref[0, rows, :seen] = rounded
        slope_ref[0, rows, :seen] = slope
        att_ref[rows] = dot_nn(rounded, v_ref[:seen]).astype(jnp.bfloat16)


def attend_call(layer, lengths, reach, q, k, v):
    length, q_width = q.shape
    heads = q_width // HD
    share = heads // (k.shape[1] // HD)
    smem = pl.BlockSpec(memory_space=pltpu.SMEM)
    own = pl.BlockSpec((length, HD), lambda h: (0, h))
    shared = pl.BlockSpec((length, HD), lambda h: (0, h // share))
    square = pl.BlockSpec((1, length, length), lambda h: (h, 0, 0))
    return pl.pallas_call(
        functools.partial(attend_kernel, layer),
        grid=(heads,),
        in_specs=[smem, smem, own, shared, shared],
        out_specs=[own, square, square],
        out_shape=[
            jax.ShapeDtypeStruct((length, q_width), jnp.bfloat16),
            jax.ShapeDtypeStruct((heads, length, length), jnp.bfloat16),
            jax.ShapeDtypeStruct((heads, length, length), jnp.float32),
        ],
        cost_estimate=pl.CostEstimate(
            flops=4 * heads * length * length * HD,
            transcendentals=2 * heads * length * length,
            bytes_accessed=6 << 20,
        ),
    )(lengths, reach, q, k, v)


def attention_kernel(layer, flat, fused, chunks, side, rank, *refs):
    g_refs, refs = (refs[: 1 if flat else 4], refs[1 if flat else 4 :])
    wo_ref, q_ref, k_ref, v_ref, rope_ref, recip_ref, wq_ref, wk_ref, wv_ref, *refs = refs
    if fused:
        lengths, reach, *refs = refs
    else:
        att_ref, prob_ref, slope_ref, *refs = refs
    shared_ref, *rest = refs
    acc, heads_ref, factor_ref, dk, dv = rest[-5:]
    others, owns = (rest[:chunks], rest[chunks : 2 * chunks])
    pieces = rest[2 * chunks : -5]
    step = pl.program_id(0)
    steps = pl.num_programs(0) // 2
    length, q_width = acc.shape
    k_width = dk.shape[1]

    @pl.when(step == 0)
    def _():
        acc[...] = jnp.zeros_like(acc)

    if flat:

        @pl.when(step < steps)
        def _():
            acc[...] += dot_nt(g_refs[0][...], wo_ref[0])

        for mask, piece in enumerate(pieces):

            @pl.when(step == mask)
            def _():
                piece[...] = g_refs[0][...]

    else:
        for mask, g_ref in enumerate(g_refs):

            @pl.when(step == mask)
            def _():
                acc[...] += dot_nt(g_ref[...], wo_ref[0])

    @pl.when(step == steps - 1)
    def _():
        cosine, sine = rope_factors(rope_ref[...])
        recip = recip_ref[:, :1]

        def unturn(part, rows):
            return part * cosine[rows] - pltpu.roll(part, HD // 2, 1) * sine[rows]

        heads_ref[...] = acc[...].astype(jnp.bfloat16)
        dk[...] = jnp.zeros_like(dk)
        dv[...] = jnp.zeros_like(dv)
        heads = q_width // HD
        share = heads // (k_width // HD)

        def head_step(head, carry):
            part = pl.ds(pl.multiple_of(head * HD, HD), HD)
            kv_part = pl.ds(pl.multiple_of((head // share) * HD, HD), HD)
            att_part = pl.ds(pl.multiple_of(q_width + 2 * k_width + head * HD, HD), HD)
            for start in range(0, length, ROW_BLOCK):
                rows, seen = (slice(start, start + ROW_BLOCK), start + ROW_BLOCK)
                ga = heads_ref[rows, part]
                if fused:
                    allowed = allowed_block(lengths, reach[layer], start, ROW_BLOCK, seen)
                    rounded, slope = weigh(q_ref[rows, part], k_ref[:seen, kv_part], allowed)
                    att = dot_nn(rounded, v_ref[:seen, kv_part]).astype(jnp.bfloat16)
                else:
                    rounded = prob_ref[head, rows, :seen]
                    slope = slope_ref[head, rows, :seen]
                    att = att_ref[rows, part]
                shared_ref[rows, att_part] = att
                delta = jnp.sum(
                    ga.astype(jnp.float32) * att.astype(jnp.float32), axis=-1, keepdims=True
                )
                grad_probs = dot_nt(ga, v_ref[:seen, kv_part])
                grad_scores = (slope * (grad_probs - delta)).astype(jnp.bfloat16)
                gq = unturn(dot_nn(grad_scores, k_ref[:seen, kv_part]), rows)
                factor_ref[rows, part] = gq.astype(jnp.bfloat16)
                shared_ref[rows, part] = (gq * recip[rows]).astype(jnp.bfloat16)
                dk[:seen, kv_part] += contract_rows(grad_scores, q_ref[rows, part])
                dv[:seen, kv_part] += contract_rows(rounded, ga)
            return carry

        lax.fori_loop(0, heads, head_step, 0)
        every = slice(0, length)
        for kv in range(k_width // HD):
            kv_part = slice(kv * HD, (kv + 1) * HD)
            part = slice(q_width + kv * HD, q_width + (kv + 1) * HD)
            gk = unturn(dk[:, kv_part], every)
            factor_ref[:, part] = gk.astype(jnp.bfloat16)
            shared_ref[:, part] = (gk * recip).astype(jnp.bfloat16)
        part = slice(q_width + k_width, q_width + 2 * k_width)
        factor_ref[:, part] = dv[...].astype(jnp.bfloat16)
        shared_ref[:, part] = (dv[...] * recip).astype(jnp.bfloat16)

    @pl.when(step >= steps)
    def _():
        rows = length // chunks
        width = wq_ref.shape[1]
        tile = width // 3

        def tile_step(turn, carry):
            here = pl.ds(pl.multiple_of(turn * tile, 128), tile)
            total = dot_nt(factor_ref[:, :q_width], wq_ref[0, here])
            total += dot_nt(factor_ref[:, q_width : q_width + k_width], wk_ref[0, here])
            total += dot_nt(
                factor_ref[:, q_width + k_width : q_width + 2 * k_width], wv_ref[0, here]
            )

            @pl.when(step < steps + steps // 2)
            def _():
                for chunk in range(chunks):
                    others[chunk][0, :, here] = total[chunk * rows : (chunk + 1) * rows].astype(
                        jnp.bfloat16
                    )

            @pl.when(step >= steps + steps // 2)
            def _():
                for chunk in range(chunks):
                    owns[chunk][0, :, here] = total[chunk * rows : (chunk + 1) * rows].astype(
                        jnp.bfloat16
                    )

            return carry

        lax.fori_loop(0, 3, tile_step, 0)


def attention_call(
    layer, steps, chunks, side, rank, upstream, w_out, q, k, v, rope, recip, w_query, w_key,
    w_value, lengths, reach, saved,
):
    length, q_width = q.shape
    k_width = k.shape[1]
    depth = w_out.shape[2]
    width = depth // steps
    flat = len(upstream) == 1
    fused = saved is None
    half = steps // 2

    def whole(*shape):
        return pl.BlockSpec(shape, lambda k, side, rank: (0,) * len(shape))

    def first(k):
        return jnp.minimum(k, steps - 1)

    def last(k, side):
        turn = jnp.maximum(k - steps, 0)
        block = turn + half * (1 - side[0])
        return jnp.where(block >= steps, block - steps, block)

    def weight(columns):
        return pl.BlockSpec((1, width, columns), lambda k, side, rank: (layer, last(k, side), 0))

    if flat:
        g_specs = [pl.BlockSpec((length, width), lambda k, side, rank: (0, first(k) ^ rank[0]))]
    else:
        g_specs = [whole(length, width)] * steps
    pieces = steps if flat else 0
    rows = length // chunks
    other_spec = pl.BlockSpec(
        (1, rows, width), lambda k, side, rank: (jnp.clip(k - steps, 0, half - 1), 0, 0)
    )
    own_spec = pl.BlockSpec(
        (1, rows, width), lambda k, side, rank: (jnp.clip(k - steps - half, 0, half - 1), 0, 0)
    )
    smem = pl.BlockSpec(memory_space=pltpu.SMEM)
    extra = [lengths, reach] if fused else list(saved)
    bf, f32 = (jnp.bfloat16, jnp.float32)
    f_width = 2 * (q_width + k_width)
    return pl.pallas_call(
        functools.partial(attention_kernel, layer, flat, fused, chunks),
        grid_spec=pltpu.PrefetchScalarGridSpec(
            num_scalar_prefetch=2,
            grid=(2 * steps,),
            in_specs=g_specs
            + [
                pl.BlockSpec(
                    (1, q_width, width), lambda k, side, rank: (layer, 0, first(k) ^ rank[0])
                ),
                whole(*q.shape),
                whole(*k.shape),
                whole(*v.shape),
                whole(length, HD),
                whole(length, HD),
                weight(q_width),
                weight(k_width),
                weight(k_width),
            ]
            + ([smem, smem] if fused else [whole(*part.shape) for part in extra]),
            out_specs=[whole(length, f_width)]
            + [other_spec] * chunks
            + [own_spec] * chunks
            + [whole(length, width)] * pieces,
            scratch_shapes=[
                pltpu.VMEM((length, q_width), f32),
                pltpu.VMEM((length, q_width), bf),
                pltpu.VMEM((length, q_width + 2 * k_width), bf),
                pltpu.VMEM((length, k_width), f32),
                pltpu.VMEM((length, k_width), f32),
            ],
        ),
        out_shape=[jax.ShapeDtypeStruct((length, f_width), bf)]
        + [jax.ShapeDtypeStruct((half, rows, width), bf)] * (2 * chunks)
        + [jax.ShapeDtypeStruct((length, width), bf)] * pieces,
        cost_estimate=pl.CostEstimate(
            flops=4 * length * depth * (q_width + k_width),
            transcendentals=0,
            bytes_accessed=20 << 20,
        ),
    )(side, rank, *upstream, w_out, q, k, v, rope, recip, w_query, w_key, w_value, *extra)


NORM_ROWS = 16


def norm_kernel(layer, flat, keep, steps, count, parts, side, rank, *refs):
    owns, others, refs = (refs[:count], refs[count : 2 * count], refs[2 * count :])
    x_ref, recip_ref, *refs = refs
    pieces = 1 if flat else steps
    g_refs, gain_ref, rest = (refs[:pieces], refs[pieces], refs[pieces + 1 :])
    outs = rest[-(1 if keep else steps) - 1 : -1]
    gain_out = rest[-1]
    halves, tile, width = owns[0].shape
    depth = steps * width
    step = pl.program_id(0)

    @pl.when(step == 0)
    def _():
        if len(rest) > len(outs) + 1:
            gain_out[...] = rest[len(outs)][...]
        else:
            gain_out[...] = jnp.zeros_like(gain_out)

    def row_step(own_ref, other_ref, turn, carry):
        rows = pl.ds(pl.multiple_of(turn * NORM_ROWS, NORM_ROWS), NORM_ROWS)
        recip = recip_ref[rows, :1]

        def grad_of(block):
            pick = jnp.broadcast_to(block // halves == side[0], (NORM_ROWS, width))
            half = block % halves
            return jnp.where(pick, own_ref[half, rows], other_ref[half, rows]).astype(jnp.float32)

        total = jnp.zeros((NORM_ROWS, HD), jnp.float32)
        for mask in range(steps):
            block = mask ^ rank[0]
            columns = pl.ds(pl.multiple_of(block * width, 128), width)
            product = grad_of(block) * x_ref[0, rows, columns].astype(jnp.float32) * recip
            gain_out[:, columns] += product[:8] + product[8:]
            weighted = product * gain_ref[layer : layer + 1, columns]
            for start in range(0, width, HD):
                total += weighted[:, start : start + HD]
        slope = recip * recip * (jnp.sum(total, axis=-1, keepdims=True) / depth)
        for mask in range(steps):
            block = mask ^ rank[0]
            columns = pl.ds(pl.multiple_of(block * width, 128), width)
            g = g_refs[0][rows, columns] if flat else g_refs[mask][rows]
            value = (
                g.astype(jnp.float32)
                + grad_of(block) * gain_ref[layer : layer + 1, columns] * recip
                - x_ref[0, rows, columns].astype(jnp.float32) * slope
            ).astype(jnp.bfloat16)
            if keep:
                outs[0][rows, columns] = value
            else:
                outs[mask][rows] = value
        return carry

    for member in range(count):

        @pl.when(step // parts == member)
        def _():
            lax.fori_loop(
                0,
                tile // NORM_ROWS,
                functools.partial(row_step, owns[member], others[member]),
                0,
            )


def norm_call(
    layer, first, side, rank, owns, others, layer_inputs, recip, upstream, gain, keep, earlier
):
    count = len(owns)
    halves, rows, width = owns[0].shape
    steps = 2 * halves
    length, depth = layer_inputs.shape[1:]
    flat = len(upstream) == 1
    tile = 32
    parts = rows // tile
    start = first * parts

    def half_spec(member):
        return pl.BlockSpec(
            (halves, tile, width), lambda r: (0, jnp.clip(r - member * parts, 0, parts - 1), 0)
        )

    flat_spec = pl.BlockSpec((tile, depth), lambda r: (start + r, 0))
    piece_spec = pl.BlockSpec((tile, width), lambda r: (start + r, 0))
    gain_spec = pl.BlockSpec((8, depth), lambda r: (0, 0))
    smem = pl.BlockSpec(memory_space=pltpu.SMEM)
    extra = [] if earlier is None else list(earlier)
    outs = 1 if keep else steps
    before = 5 + 2 * count + len(upstream)
    return pl.pallas_call(
        functools.partial(norm_kernel, layer, flat, keep, steps, count, parts),
        grid=(count * parts,),
        in_specs=[smem, smem]
        + [half_spec(member) for member in range(count)] * 2
        + [
            pl.BlockSpec((1, tile, depth), lambda r: (layer, start + r, 0)),
            pl.BlockSpec((tile, HD), lambda r: (start + r, 0)),
        ]
        + [flat_spec if flat else piece_spec] * len(upstream)
        + [pl.BlockSpec(gain.shape, lambda r: (0, 0))]
        + ([pl.BlockSpec(memory_space=pl.ANY)] * outs + [gain_spec])[: len(extra)],
        out_specs=[flat_spec if keep else piece_spec] * outs + [gain_spec],
        out_shape=[
            jax.ShapeDtypeStruct((length, depth) if keep else (length, width), jnp.bfloat16)
        ]
        * outs
        + [jax.ShapeDtypeStruct((8, depth), jnp.float32)],
        input_output_aliases={before + i: i for i in range(outs)} if extra else {},
        cost_estimate=pl.CostEstimate(
            flops=30 * count * rows * depth, transcendentals=0, bytes_accessed=4 * count << 20
        ),
    )(side, rank, *owns, *others, layer_inputs, recip, *upstream, gain, *extra)


def weights_kernel(count, groups, *refs):
    normed = refs[:count]
    upstream = refs[count : 2 * count]
    factors = refs[2 * count : 3 * count]
    wq_ref, wk_ref, wv_ref, wo_ref = refs[-4:]
    q_width, k_width = (wq_ref.shape[2], wk_ref.shape[2])
    widths = (q_width, k_width, k_width)
    start = 0
    for out_ref, width in zip((wq_ref, wk_ref, wv_ref), widths):
        total = 0.0
        for member in range(count):
            total += contract_rows(normed[member][...], factors[member][:, start : start + width])
        out_ref[0] = total / groups
        start += width
    total = 0.0
    for member in range(count):
        total += contract_rows(factors[member][:, start:], upstream[member][...])
    wo_ref[0] = total / groups


def weights_call(
    layer, layers, normed, upstream, factors, q_width, k_width, earlier, first_tile, tiles
):
    count = len(normed)
    length, width = normed[0].shape
    tile = width // 3
    piece = pl.BlockSpec((length, tile), lambda n: (0, n + first_tile))
    factor = pl.BlockSpec(factors[0].shape, lambda n: (0, 0))
    any_spec = pl.BlockSpec(memory_space=pl.ANY)
    extra = [] if earlier is None else list(earlier)
    f32 = jnp.float32

    def tall(columns):
        return pl.BlockSpec((1, tile, columns), lambda n: (layer, n + first_tile, 0))

    return pl.pallas_call(
        functools.partial(weights_kernel, count, count),
        grid=(tiles,),
        in_specs=[piece] * (2 * count) + [factor] * count + [any_spec] * len(extra),
        out_specs=[
            tall(q_width),
            tall(k_width),
            tall(k_width),
            pl.BlockSpec((1, q_width, tile), lambda n: (layer, 0, n + first_tile)),
        ],
        out_shape=[
            jax.ShapeDtypeStruct((layers, width, q_width), f32),
            jax.ShapeDtypeStruct((layers, width, k_width), f32),
            jax.ShapeDtypeStruct((layers, width, k_width), f32),
            jax.ShapeDtypeStruct((layers, q_width, width), f32),
        ],
        input_output_aliases={3 * count + i: i for i in range(len(extra))},
        cost_estimate=pl.CostEstimate(
            flops=4 * count * length * tile * tiles * (q_width + k_width),
            transcendentals=0,
            bytes_accessed=8 * tiles << 20,
        ),
    )(*normed, *upstream, *factors, *extra)


def xor_send(x, axis, mask):
    return lax.ppermute(x, axis, [(i, i ^ mask) for i in range(lax.axis_size(axis))])


def spread_pieces(pieces):
    return [pieces[0]] + [
        xor_send(piece, "dp", mask)
        for mask, piece in enumerate(pieces)
        if mask
    ]


def share_factor(factor):
    beside = xor_send(factor, "dp", 1)
    across = xor_send(factor, "dp", 2)
    return [beside, across]


def along_line(x, pairs):
    return lax.ppermute(
        x, "tp", [(2 * a + side, 2 * b + side) for a, b in pairs for side in range(2)]
    )


def rounded_sum(left, right):
    return (left.astype(jnp.float32) + right.astype(jnp.float32)).astype(jnp.bfloat16)


def after(value, *earlier):
    return lax.optimization_barrier((value, *earlier))[0]


def wave_order(chunks):
    order = []
    for slot in range(chunks + 3):
        order += [(stage, slot - stage) for stage in range(4) if 0 <= slot - stage < chunks]
    return order + [(4, 0), (4, chunks - 1)]


class Wave:
    def __init__(self, sent, kept, outer):
        self.outer = outer
        self.value = list(kept)
        self.moved = [xor_send(part, "tp", 1) for part in sent]
        self.last = None

    def tie(self, value):
        return value if self.last is None else after(value, self.last)

    def step(self, chunk, stage):
        value, moved = (self.value[chunk], self.tie(self.moved[chunk]))
        if stage == 3:
            value = jnp.where(self.outer, moved, value)
        else:
            value = rounded_sum(value, moved)
        self.value[chunk] = self.last = value
        if stage == 0:
            self.moved[chunk] = along_line(value, [(0, 1), (3, 2)])
        elif stage == 1:
            self.moved[chunk] = along_line(value, [(1, 2), (2, 1)])
        elif stage == 2:
            self.moved[chunk] = along_line(value, [(1, 0), (2, 3)])
        else:
            self.moved[chunk] = xor_send(value, "tp", 1)


def local(layer_inputs, out_grad, gain, w_query, w_key, w_value, w_out, doc_lengths, window_reach):
    if w_query.shape[2] == HD or lax.axis_size("dp") != 4 or lax.axis_size("tp") != 8:
        return local_general(
            layer_inputs, out_grad, gain, w_query, w_key, w_value, w_out, doc_lengths, window_reach
        )
    count = lax.axis_size("dp")
    rank = lax.axis_index("dp").astype(jnp.int32).reshape(1)
    chunks = CHUNKS
    layers = layer_inputs.shape[0]
    length = layer_inputs.shape[1]
    q_width, k_width = (w_query.shape[2], w_key.shape[2])
    rope = rope_wide(length, HD)
    normed = [None] * layers
    place = lax.axis_index("tp")
    side = (place % 2).astype(jnp.int32).reshape(1)
    line = place // 2
    outer = (line == 0) | (line == 3)

    grads = None
    gains = [None] * layers
    top = layers - 1
    waiting = None
    upstream = [out_grad]

    def project(layer, inputs):
        result = project_call(
            layer, count, rank, inputs, gain, w_query, w_key, w_value, rope
        )
        return (result[:count], result[count : count + 3], result[-1])

    def weights(layer, factors, sent, tie, first_tile=0, tiles=3):
        sent = [after(sent[0], tie)] + sent[1:]
        return weights_call(
            layer, layers, normed[layer], sent, factors, q_width, k_width, grads, first_tile,
            tiles,
        )

    pieces, heads, recip = project(top, layer_inputs)
    normed[top] = spread_pieces(pieces)
    saved = None
    for layer in reversed(range(layers)):
        factor, *partial = attention_call(
            layer, count, chunks, side, rank, upstream, w_out, *heads, rope, recip, w_query,
            w_key, w_value, doc_lengths, window_reach, saved,
        )
        wave = Wave(partial[:chunks], partial[chunks : 2 * chunks], outer)
        owned = partial[2 * chunks :] or upstream
        if layer:
            wave.last = after(layer_inputs, factor)
            next_pieces, next_heads, next_recip = project(layer - 1, wave.last)
            wave.last = next_heads[0]
        if waiting is not None:
            grads = weights(*waiting, factor)
            wave.last = grads[1]
        result = None
        for stage, chunk in wave_order(chunks):
            if stage < 4:
                wave.step(chunk, stage)
            else:
                members = range(chunk, chunks - 1) if chunk < chunks - 1 else range(chunk, chunks)
                result = norm_call(
                    layer, chunk, side, rank, [wave.value[member] for member in members],
                    [wave.tie(wave.moved[member]) for member in members], layer_inputs, recip,
                    upstream, gain, layer == 0, result,
                )
                wave.last = result[-1]
            if (stage, chunk) == (0, 0):
                tied = owned
                if layer == top:
                    tied = [
                        after(piece, wave.last) if mask else piece
                        for mask, piece in enumerate(owned)
                    ]
                factors = [factor] + share_factor(after(factor, wave.last))
                sent = spread_pieces(tied)
            if layer and (stage, chunk) == (0, 1):
                tied = [
                    after(piece, wave.last) if mask else piece
                    for mask, piece in enumerate(next_pieces)
                ]
                normed[layer - 1] = spread_pieces(tied)
            if (stage, chunk) == (2, chunks - 1):
                factors.append(xor_send(after(factors[2], wave.last), "dp", 1))
            if (stage, chunk) == (3, chunks - 2):
                if layer:
                    saved = attend_call(
                        layer - 1, doc_lengths, window_reach, wave.tie(next_heads[0]),
                        *next_heads[1:],
                    )
                    wave.last = saved[0]
                else:
                    grads = weights(layer, factors, sent, wave.last, 0, 2)
                    wave.last = grads[1]
        *upstream, gain_part = result
        waiting = (layer, factors, sent)
        if layer:
            heads, recip = (next_heads, next_recip)
        gains[layer] = gain_part
    grads = weights(*waiting, gain_part, 2, 1)
    gain_rows = jnp.stack([jnp.sum(part, axis=0) for part in lax.optimization_barrier(gains)])
    beside, across, corner = (
        xor_send(gain_rows, "dp", mask) for mask in range(1, 4)
    )
    gain_total = ((gain_rows + beside) + (across + corner)) / count
    return (upstream[0], *grads, gain_total)


def solution(mesh):
    in_specs = (
        P(None, "dp", None),
        P("dp", None),
        P(),
        P(None, None, "tp"),
        P(None, None, "tp"),
        P(None, None, "tp"),
        P(None, "tp", None),
        P("dp", None),
        P(),
    )
    out_specs = (
        P("dp", None),
        P(None, "dp", "tp"),
        P(None, "dp", "tp"),
        P(None, "dp", "tp"),
        P(None, "tp", "dp"),
        P(),
    )

    return jax.shard_map(local, mesh=mesh, in_specs=in_specs, out_specs=out_specs, check_vma=False)
```
